512 devices in a mesh: row: 32 (over y, z_lo, core), col: 16 (over z_hi, x).
Axes of the slice: x: 4, y: 4, z: 16 (z_hi: 4, z_lo: 4; z = z_hi * 4 + z_lo), core: 2. Of those that a mesh axis runs over, the one named last changes fastest.
Arguments:
- tokens: bfloat16 [5120, 2048], P('row', 'col'), may hold values from -1600 to 1600, as said below
- norm_gain: float32 [2048], P('col'), may hold values from 0.1 to 1.9
- lengths: int32 [16], replicated, may hold values from 1 to 1280, 5120 in all
- request_adapter: int32 [16], replicated, may hold values from 0 to 63
- routes: int32 [5120, 2], P('row'), may hold values from 0 to 7, all different within a row; in each aligned block of 160 rows (0 to 159, 160 to 319, ...) at most 60 rows name the same one
- route_weights: float32 [5120, 2], P('row'), may hold values from 0.2 to 1
- gate_weight: bfloat16 [32, 1408, 2048], P('row', 'col'), may hold values from -0.125 to 0.125
- up_weight: bfloat16 [32, 1408, 2048], P('row', 'col'), may hold values from -0.125 to 0.125
- down_weight: bfloat16 [32, 1408, 2048], P('row', None, 'col'), may hold values from -0.078125 to 0.078125
- adapter_down: bfloat16 [64, 2048, 16], P('row', 'col'), may hold values from -0.125 to 0.125
- adapter_up: bfloat16 [64, 16, 2048], P('row', None, 'col'), may hold values from -1.5 to 1.5
Outputs:
- mixed: bfloat16 [5120, 2048], P('row', 'col')
The draws below stay inside these ranges and needn't reach their ends.
Inputs may be any that keep to these rules, and one draw needn't show every extreme that they name: Feature scales differ over the features and token scales over the tokens. The lengths sum to 5120. `routes`: A token's two experts differ. Among the tokens of one index of row (aligned blocks of 160 tokens) no expert is named by more than 60 tokens, a bound that some block reaches.
All inputs are finite; a program needn't handle non-finite values.
Results may differ from the reference program's by a relative error of at most 0.008.
Values may be sent and summed in bfloat16 or wider, within the bound.
A program may use at most 64 MiB of HBM per device.

```python
import math
import jax
import jax.numpy as jnp
import numpy as np
from jax import lax

D = 2048
FF = 5632
EXPERTS = 8
TOPK = 2
RANK = 16
ADAPTERS = 64
REQUESTS = 16
TOK_DEV = 160
TOKENS = 5120
UNITS = 32
UNIT_FF = 1408
CAP = 60
N_ROW = 32


def draw_tokens(key, part):
    first_key, second_key, third_key = jax.random.split(jax.random.fold_in(key, 11), 3)
    feature_scale = 10.0 ** (jnp.arange(D, dtype=jnp.float32) / D) * jnp.exp(jax.random.uniform(second_key, (D,), jnp.float32, -0.5, 0.5))
    base = jnp.clip(jax.random.normal(first_key, (TOKENS, D), jnp.float32), -6.0, 6.0)
    token_scale = jnp.exp(jax.random.uniform(third_key, (TOKENS, 1), jnp.float32, 0.0, math.log(10.0)))
    return (base * feature_scale[None, :] * token_scale).astype(jnp.bfloat16)


def set_ends(values, key, low, largest):
    place = [jax.random.randint(jax.random.fold_in(key, axis), (), 0, length) for axis, length in enumerate(values.shape)]
    widest = values.shape.index(max(values.shape))
    next_to = place[:widest] + [(place[widest] + 1) % values.shape[widest]] + place[widest + 1:]
    return values.at[tuple(place)].set(low).at[tuple(next_to)].set(largest)


def block_levels(rng, shape, pieces, least, top_value):
    level, own = 1.0, jax.random.fold_in(rng, 6)
    for axis_at, shards_of in pieces:
        heights = jnp.exp(jax.random.uniform(jax.random.fold_in(own, axis_at), (shards_of,), jnp.float32, least / len(pieces), top_value / len(pieces)))
        level = level * jnp.repeat(heights, shape[axis_at] // shards_of).reshape([-1 if axis == axis_at else 1 for axis in range(len(shape))])
    return level


def split_up(amount, total, bound, skew):
    loads = [(1 << 20) // math.isqrt(standing ** skew) + 1 for standing in range(2, amount + 1)]
    rest, counts = total - bound - (amount - 1), [1] * (amount - 1)
    while rest > 0:
        candidates = [i for i in range(amount - 1) if counts[i] < bound]
        pool, remaining = sum([loads[i] for i in candidates]), rest
        for i in candidates:
            extra = min(bound - counts[i], max(1, remaining * loads[i] // pool), rest)
            counts[i] = counts[i] + extra
            rest = rest - extra
    return np.array([bound] + counts)


def uneven_parts(rng, count, total, most, slope):
    if count == 2:
        one = jax.random.randint(rng, (), max(1, total - most), min(most, total - 1) + 1)
        return jnp.stack([one, total - one])
    tallies = jnp.asarray(split_up(count, total, most, slope), jnp.int32)
    couples = (count - 1) // 2
    donor, sink = tallies[1:1 + 2 * couples:2], tallies[2:2 + 2 * couples:2]
    room = jnp.minimum(donor - 1, most - sink)
    moved = jax.random.randint(jax.random.fold_in(rng, 1), (couples,), 0, 1 << 20) % (room + 1)
    tallies = tallies.at[1:1 + 2 * couples:2].set(donor - moved).at[2:2 + 2 * couples:2].set(sink + moved)
    return tallies[jax.random.permutation(jax.random.fold_in(rng, 2), count)]


def shared_out(own_key, own, number, rows, amount, top, bound, slope):
    sequence = jax.random.permutation(own_key, amount)
    heavy_load, usual = portions_of(amount, rows * top, bound, slope, True), portions_of(amount, rows * top, bound, slope, False)
    places = jnp.arange(amount)

    def named(tallies, offset_by):
        used = int((tallies > 0).sum())
        fixed = max(1, used // 4)
        passed = fixed + (places - fixed + offset_by * (used - fixed)) % max(1, amount - fixed)
        return jnp.zeros((amount,), jnp.int32).at[sequence[jnp.where(places < fixed, places, passed)]].set(jnp.asarray(tallies, jnp.int32))

    tallies = jnp.where(number % 4 == 0, named(heavy_load, number // 4), named(usual, number - number // 4 - 1))
    mixed = jax.random.permutation(jax.random.fold_in(own, 3), amount)
    source_of, receiver = mixed[0:amount // 2 * 2:2], mixed[1:amount // 2 * 2:2]
    margin = jnp.minimum(tallies[source_of] - 1, bound - tallies[receiver]) // 2
    margin = jnp.where((source_of == sequence[0]) | (receiver == sequence[0]) | (tallies[receiver] == 0), 0, jnp.maximum(margin, 0))
    passed = jax.random.randint(jax.random.fold_in(own, 4), (amount // 2,), 0, 1 << 20) % (margin + 1)
    tallies = tallies.at[source_of].add(-passed).at[receiver].add(passed)
    items = jnp.searchsorted(jnp.cumsum(tallies), jnp.arange(rows * top), side="right").astype(jnp.int32)
    listing = items.reshape(top, rows).T
    listing = listing[jax.random.permutation(jax.random.fold_in(own, 1), rows)]
    offset_by = jax.random.randint(jax.random.fold_in(own, 2), (rows, 1), 0, top)
    return jnp.take_along_axis(listing, (jnp.arange(top)[None, :] + offset_by) % top, axis=1)


def portions_of(amount, total, most, slope, full):
    portions = [(1 << 20) // math.isqrt(standing ** slope) + 1 for standing in range(1, amount + 1)]
    largest = most if full else min(most, max(-(-total // amount), total * portions[0] // sum(portions)))
    least = 1 if total - largest >= amount - 1 else 0
    given, spare = [largest] + [least] * (amount - 1), total - largest - least * (amount - 1)
    while spare > 0:
        free = [i for i in range(1, amount) if given[i] < largest] or [i for i in range(1, amount) if given[i] < most]
        pool, remaining = sum([portions[i] for i in free]), spare
        for i in free:
            addition = min(most - given[i], max(1, remaining * portions[i] // pool), spare)
            given[i] = given[i] + addition
            spare = spare - addition
    return np.array(given)


def scatter_about(stream_key, extent, deviation, reach, cuts=(), kind=jnp.bfloat16):
    values = jax.random.normal(stream_key, extent, jnp.float32) * deviation
    if len(cuts) > 0:
        values = block_levels(stream_key, extent, cuts, -0.22, 0.18) * values
    return jnp.clip(values, min=-reach, max=reach).astype(kind)


def setup_inputs(seed: int = 0) -> dict:
    key_of = jax.random.split(jax.random.key(seed), 12)
    tokens = draw_tokens(jax.random.fold_in(key_of[11], 71), 0)
    norm_gain = jnp.clip(1.0 + 0.18 * jax.random.normal(key_of[1], (D,), jnp.float32), 0.1, 1.9)
    lengths = uneven_parts(key_of[2], REQUESTS, TOKENS, TOKENS // 4, 2).astype(jnp.int32)
    request_adapter = set_ends(jax.random.randint(key_of[3], (REQUESTS,), 0, ADAPTERS), jax.random.fold_in(key_of[3], 1), 0, ADAPTERS - 1).astype(jnp.int32)
    routes_keys = jax.random.split(jax.random.fold_in(key_of[4], 1), TOKENS // TOK_DEV)
    routes_turns = jax.random.permutation(jax.random.fold_in(key_of[4], 3), TOKENS // TOK_DEV)
    routes = jax.vmap(lambda own, number: shared_out(jax.random.fold_in(key_of[4], 2), own, number, TOK_DEV, EXPERTS, TOPK, CAP, 2))(routes_keys, routes_turns).reshape((TOKENS, TOPK))
    route_weights = jnp.clip(0.2 + 0.8 * jax.random.uniform(key_of[5], (TOKENS, TOPK), jnp.float32) ** block_levels(key_of[5], (TOKENS, TOPK), ((0, 32),), -0.2, 0.2), 0.2, 1.0)
    gate_weight = scatter_about(key_of[6], (UNITS, UNIT_FF, D), D ** -0.5, 0.125, ((0, 32), (1, 16)))
    up_weight = scatter_about(key_of[7], (UNITS, UNIT_FF, D), D ** -0.5, 0.125, ((0, 32), (1, 16)))
    down_weight = scatter_about(key_of[8], (UNITS, UNIT_FF, D), FF ** -0.5, 0.078125, ((0, 32), (2, 16)))
    adapter_down = scatter_about(key_of[9], (ADAPTERS, D, RANK), D ** -0.5, 0.125, ((0, 32), (1, 16)))
    adapter_up = scatter_about(key_of[10], (ADAPTERS, RANK, D), RANK ** -0.5, 1.5, ((0, 32), (2, 16)))
    return dict(tokens=tokens, norm_gain=norm_gain, lengths=lengths, request_adapter=request_adapter, routes=routes, route_weights=route_weights, gate_weight=gate_weight, up_weight=up_weight, down_weight=down_weight, adapter_down=adapter_down, adapter_up=adapter_up)


def reference(tokens, norm_gain, lengths, request_adapter, routes, route_weights, gate_weight, up_weight, down_weight, adapter_down, adapter_up):
    splits = N_ROW // EXPERTS
    widened = tokens.astype(jnp.float32)
    mean_square = lax.optimization_barrier(jnp.mean(widened * widened, axis=1, keepdims=True))
    normed = (widened * lax.rsqrt(mean_square + 1e-06) * norm_gain[None, :]).astype(jnp.bfloat16)
    req_ends = jnp.cumsum(lengths)
    position = jnp.arange(TOKENS, dtype=jnp.int32)
    request = lax.optimization_barrier(jnp.sum((position[:, None] >= req_ends[None, :]).astype(jnp.int32), axis=1))
    adapter = request_adapter[request]
    select = (adapter[:, None] == jnp.arange(ADAPTERS, dtype=jnp.int32)[None, :]).astype(jnp.float32)
    down_matrix = jnp.transpose(adapter_down, (1, 0, 2)).reshape(D, ADAPTERS * RANK)
    projected = jnp.dot(normed, down_matrix, preferred_element_type=jnp.float32).reshape(TOKENS, ADAPTERS, RANK)
    low_rank = lax.optimization_barrier(jnp.sum(projected * select[:, :, None], axis=1)).astype(jnp.bfloat16)
    expanded = (select.astype(jnp.bfloat16)[:, :, None] * low_rank[:, None, :]).reshape(TOKENS, ADAPTERS * RANK)
    branch = jnp.dot(expanded, adapter_up.reshape(ADAPTERS * RANK, D), preferred_element_type=jnp.float32)
    gate_full = jnp.transpose(gate_weight.reshape(EXPERTS, splits, UNIT_FF, D), (0, 3, 1, 2)).reshape(EXPERTS, D, FF)
    up_full = jnp.transpose(up_weight.reshape(EXPERTS, splits, UNIT_FF, D), (0, 3, 1, 2)).reshape(EXPERTS, D, FF)
    down_blocks = down_weight.reshape(EXPERTS, splits, UNIT_FF, D)
    matches = (routes[:, :, None] == jnp.arange(EXPERTS, dtype=jnp.int32)[None, None, :]).astype(jnp.float32)
    combine = lax.optimization_barrier(jnp.sum(matches * route_weights[:, :, None], axis=1))

    def scan_step(running, stacked):
        gate_mat, up_mat, down_mat, weight_col = stacked
        gate_sum = jnp.dot(normed, gate_mat, preferred_element_type=jnp.float32)
        up_sum = jnp.dot(normed, up_mat, preferred_element_type=jnp.float32)
        hidden = (jax.nn.silu(gate_sum) * up_sum).astype(jnp.bfloat16)
        hidden_blocks = hidden.reshape(TOKENS, splits, UNIT_FF).astype(jnp.float32)
        block_out = jnp.einsum('tqf,qfd->tqd', hidden_blocks, down_mat.astype(jnp.float32)).astype(jnp.bfloat16)
        expert_out = lax.optimization_barrier(jnp.sum(block_out.astype(jnp.float32), axis=1))
        return (running + weight_col[:, None] * expert_out, None)
    moe_sum, unused = lax.scan(scan_step, jnp.zeros((TOKENS, D), jnp.float32), (gate_full, up_full, down_blocks, combine.T))
    return (moe_sum + branch).astype(jnp.bfloat16)
```

```python
import functools

import jax
import jax.numpy as jnp
from jax import lax
from jax.experimental import pallas as pl
from jax.experimental.pallas import tpu as pltpu
from jax.sharding import PartitionSpec as P

D = 2048
EXPERTS = 8
TOPK = 2
RANK = 16
CAP = 60
SLOTS = 64
RING = 4
UNITS_PAD = 96
MESH = pl.DeviceIdType.MESH
VMEM = pl.BlockSpec(memory_space=pltpu.VMEM)


def greet(peers):
    barrier = pltpu.get_barrier_semaphore()
    for row, col in peers:
        pl.semaphore_signal(barrier, inc=1, device_id=(row, col), device_id_type=MESH)
    pl.semaphore_wait(barrier, len(peers))


def small_kernel(n_row, n_col, sq_ref, ad_ref, sq_all, ad_all, send, local, sq_sem, ad_sem):
    r, c = lax.axis_index("row"), lax.axis_index("col")
    row_peers = [lax.rem(r + k, n_row) for k in range(1, n_row)]
    col_peers = [lax.rem(c + k, n_col) for k in range(1, n_col)]
    greet([(r, p) for p in col_peers] + [(p, c) for p in row_peers])
    own = [
        pltpu.make_async_copy(sq_ref, sq_all.at[c], local.at[0]),
        pltpu.make_async_copy(ad_ref, ad_all.at[r], local.at[1]),
    ]
    sends = []
    for p in col_peers:
        sends.append(
            pltpu.make_async_remote_copy(
                sq_ref, sq_all.at[c], send.at[len(sends)], sq_sem.at[c], (r, p), MESH
            )
        )
    for p in row_peers:
        sends.append(
            pltpu.make_async_remote_copy(
                ad_ref, ad_all.at[r], send.at[len(sends)], ad_sem.at[r], (p, c), MESH
            )
        )
    for copy in sends + own:
        copy.start()
    for copy in own:
        copy.wait()
    for p in col_peers:
        pltpu.make_async_copy(sq_ref, sq_all.at[p], sq_sem.at[p]).wait()
    for p in row_peers:
        pltpu.make_async_copy(ad_ref, ad_all.at[p], ad_sem.at[p]).wait()
    for copy in sends:
        copy.wait_send()


def small_exchange(sq, ad, n_row, n_col):
    return pl.pallas_call(
        functools.partial(small_kernel, n_row, n_col),
        out_shape=(
            jax.ShapeDtypeStruct((n_col,) + sq.shape, sq.dtype),
            jax.ShapeDtypeStruct((n_row,) + ad.shape, ad.dtype),
        ),
        in_specs=[VMEM] * 2,
        out_specs=(VMEM,) * 2,
        scratch_shapes=[
            pltpu.SemaphoreType.DMA((n_row + n_col,)),
            pltpu.SemaphoreType.DMA((2,)),
            pltpu.SemaphoreType.DMA((n_col,)),
            pltpu.SemaphoreType.DMA((n_row,)),
        ],
        compiler_params=pltpu.CompilerParams(collective_id=0, has_side_effects=True),
    )(sq, ad)


def main_kernel(
    n_row,
    buf_ref,
    low_ref,
    w_ref,
    wd_ref,
    ret_ref,
    lowsum_ref,
    toks,
    hid,
    lowz,
    lowmid,
    lowx,
    osend,
    orecv,
    oacc,
    rbuf,
    send,
    local,
    d_sem,
    t_sem,
    p_sem,
    h_sem,
    lz_sem,
    lx_sem,
    o_sem,
    r_sem,
):
    r, c = lax.axis_index("row"), lax.axis_index("col")
    core, half_row = r % 2, r // 2
    other = 1 - core
    partner = r + 1 - 2 * core
    zh, xx = c // RING, c % RING
    pairs = n_row // 2
    rows_half = pairs * SLOTS
    piece = rows_half // 2

    def col_of(z, x):
        return (z % RING) * RING + x % RING

    z_right, z_left, z_far = col_of(zh + 1, xx), col_of(zh + 3, xx), col_of(zh + 2, xx)
    x_right, x_left, x_far = col_of(zh, xx + 1), col_of(zh, xx + 3), col_of(zh, xx + 2)
    row_steps = [(half_row + k) % pairs for k in range(1, pairs)]
    greet(
        [(2 * i + core, c) for i in row_steps]
        + [(r, p) for p in (z_right, z_left, z_far, x_right, x_left, x_far)]
        + [(partner, c)]
    )
    sends = []

    def push(src, dst, recv, row, col):
        copy = pltpu.make_async_remote_copy(
            src, dst, send.at[len(sends)], recv, (row, col), MESH
        )
        copy.start()
        sends.append(copy)

    def arrived(ref, recv):
        pltpu.make_async_copy(ref, ref, recv).wait()

    def expert_of(i):
        return (2 * i + core) // 4

    own = pltpu.make_async_copy(
        buf_ref.at[expert_of(half_row)],
        toks.at[core, c, pl.ds(half_row * SLOTS, SLOTS)],
        local.at[0],
    )
    own.start()
    for i in row_steps:
        push(
            buf_ref.at[expert_of(i)],
            toks.at[core, c, pl.ds(half_row * SLOTS, SLOTS)],
            d_sem.at[half_row],
            2 * i + core,
            c,
        )
    for p in (z_right, z_left, z_far):
        push(low_ref, lowz.at[zh], lz_sem.at[zh], r, p)
    own.wait()
    for i in row_steps:
        arrived(toks.at[core, c, pl.ds(i * SLOTS, SLOTS)], d_sem.at[i])

    def gather(piece_of, sem, done):
        def go(col, part, to):
            push(piece_of(col, part), piece_of(col, part), sem.at[col * 2 + part], r, to)

        def got(col, part):
            arrived(piece_of(col, part), sem.at[col * 2 + part])

        def fan_x(col, part):
            go(col, part, x_right)
            go(col, part, x_left)

        def relay_x(z):
            from_left, from_right, far = col_of(z, xx + 3), col_of(z, xx + 1), col_of(z, xx + 2)
            got(from_left, 0)
            go(from_left, 0, x_right)
            got(from_right, 1)
            go(from_right, 1, x_left)
            got(from_left, 1)
            done(from_left)
            got(from_right, 0)
            done(from_right)
            return far

        def finish(far):
            got(far, 0)
            got(far, 1)
            done(far)

        def first(part):
            go(c, part, z_right)
            go(c, part, z_left)
            fan_x(c, part)

        def rest():
            far_0 = relay_x(zh)
            got(z_left, 0)
            go(z_left, 0, z_right)
            fan_x(z_left, 0)
            got(z_right, 1)
            go(z_right, 1, z_left)
            fan_x(z_right, 1)
            got(z_left, 1)
            fan_x(z_left, 1)
            done(z_left)
            got(z_right, 0)
            fan_x(z_right, 0)
            done(z_right)
            finish(far_0)
            far_1 = relay_x(zh + 3)
            far_2 = relay_x(zh + 1)
            got(z_far, 0)
            fan_x(z_far, 0)
            got(z_far, 1)
            fan_x(z_far, 1)
            done(z_far)
            finish(far_1)
            finish(far_2)
            finish(relay_x(zh + 2))

        return first, rest

    def share(col):
        push(toks.at[core, col], toks.at[core, col], p_sem.at[col], partner, c)

    tok_first, tok_rest = gather(
        lambda col, part: toks.at[core, col, pl.ds(part * piece, piece)], t_sem, share
    )
    tok_first(0)
    tok_first(1)
    share(c)
    total = low_ref[...]
    for k in range(1, RING):
        z = (zh + k) % RING
        arrived(lowz.at[z], lz_sem.at[z])
        total = total + lowz[z]
    lowmid[...] = total
    for p in (x_right, x_left, x_far):
        push(lowmid, lowx.at[xx], lx_sem.at[xx], r, p)
    tok_rest()
    for k in range(1, RING):
        x = (xx + k) % RING
        arrived(lowx.at[x], lx_sem.at[x])
        total = total + lowx[x]
    lowsum_ref[...] = total

    n_col = RING * RING
    step = 256
    chunks = rows_half // step

    def hidden_of(parity):
        def one(k, carry):
            at = pl.multiple_of(k * step, step)
            x = jnp.concatenate(
                [toks[parity, col, pl.ds(at, step), :] for col in range(n_col)], axis=1
            )
            both = lax.dot_general(
                w_ref[...], x, (((1,), (1,)), ((), ())), preferred_element_type=jnp.float32
            )
            gate, up = both[:UNITS_PAD], both[UNITS_PAD:]
            hid[parity, c, :, pl.ds(at, step)] = (gate / (1.0 + jnp.exp(-gate)) * up).astype(
                jnp.bfloat16
            )
            return carry

        lax.fori_loop(0, chunks, one, 0)

    hid_first, hid_rest = gather(
        lambda col, part: hid.at[core if part == 0 else other, col], h_sem, lambda col: None
    )
    hidden_of(core)
    hid_first(0)
    for k in range(n_col):
        arrived(toks.at[other, k], p_sem.at[k])
    hidden_of(other)
    hid_first(1)
    hid_rest()

    def out_of(parity, into):
        def one(k, carry):
            at = pl.multiple_of(k * step, step)
            h = hid[parity, :, :, pl.ds(at, step)].reshape(n_col * UNITS_PAD, step)
            y = jnp.dot(wd_ref[...], h, preferred_element_type=jnp.float32)
            into[pl.ds(at, step), :] = jnp.transpose(y).astype(into.dtype)
            return carry

        lax.fori_loop(0, chunks, one, 0)

    out_of(other, osend)
    push(osend, orecv, o_sem.at[0], partner, c)
    out_of(core, oacc)
    arrived(orecv, o_sem.at[0])
    rbuf[...] = (oacc[...] + orecv[...].astype(jnp.float32)).astype(jnp.bfloat16)
    back = pltpu.make_async_copy(
        rbuf.at[pl.ds(half_row * SLOTS, SLOTS)], ret_ref.at[half_row], local.at[1]
    )
    back.start()
    for i in row_steps:
        push(
            rbuf.at[pl.ds(i * SLOTS, SLOTS)],
            ret_ref.at[half_row],
            r_sem.at[half_row],
            2 * i + core,
            c,
        )
    back.wait()
    for i in row_steps:
        arrived(ret_ref.at[i], r_sem.at[i])
    for copy in sends:
        copy.wait_send()


def main_exchange(buffer, low, weights, down, n_row, n_col):
    pairs = n_row // 2
    rows_half = pairs * SLOTS
    width = buffer.shape[-1]
    dma = pltpu.SemaphoreType.DMA
    sends = 2 * (pairs - 1) + 6 + 2 * 30 + n_col + 1
    return pl.pallas_call(
        functools.partial(main_kernel, n_row),
        out_shape=(
            jax.ShapeDtypeStruct((pairs, SLOTS, width), jnp.bfloat16),
            jax.ShapeDtypeStruct(low.shape, jnp.float32),
        ),
        in_specs=[VMEM] * 4,
        out_specs=(VMEM,) * 2,
        scratch_shapes=[
            pltpu.VMEM((2, n_col, rows_half, width), jnp.bfloat16),
            pltpu.VMEM((2, n_col, UNITS_PAD, rows_half), jnp.bfloat16),
            pltpu.VMEM((RING,) + low.shape, jnp.float32),
            pltpu.VMEM(low.shape, jnp.float32),
            pltpu.VMEM((RING,) + low.shape, jnp.float32),
            pltpu.VMEM((rows_half, width), jnp.bfloat16),
            pltpu.VMEM((rows_half, width), jnp.bfloat16),
            pltpu.VMEM((rows_half, width), jnp.float32),
            pltpu.VMEM((rows_half, width), jnp.bfloat16),
            dma((sends,)),
            dma((2,)),
            dma((pairs,)),
            dma((2 * n_col,)),
            dma((n_col,)),
            dma((2 * n_col,)),
            dma((RING,)),
            dma((RING,)),
            dma((1,)),
            dma((pairs,)),
        ],
        compiler_params=pltpu.CompilerParams(collective_id=1, has_side_effects=True),
    )(buffer, low, weights, down)


def body(
    tokens,
    norm_gain,
    lengths,
    request_adapter,
    routes,
    route_weights,
    gate_weight,
    up_weight,
    down_weight,
    adapter_down,
    adapter_up,
):
    tok_rows, width_part = tokens.shape
    n_row, n_col = lax.axis_size("row"), lax.axis_size("col")
    widened = tokens.astype(jnp.float32)
    own_squares = jnp.sum(widened * widened, axis=1)[None, :]
    own_factors = jnp.concatenate(
        [
            jnp.transpose(adapter_down, (0, 2, 1)).reshape(-1, width_part),
            adapter_up.reshape(-1, width_part),
        ],
        axis=0,
    )
    all_squares, all_factors = small_exchange(own_squares, own_factors, n_row, n_col)
    squares = jnp.sum(all_squares, axis=(0, 1))
    normed = (widened * lax.rsqrt(squares[:, None] / D + 1e-06) * norm_gain[None, :]).astype(
        jnp.bfloat16
    )
    req_ends = jnp.cumsum(lengths)
    position = lax.axis_index("row") * tok_rows + jnp.arange(tok_rows, dtype=jnp.int32)
    request = jnp.sum((position[:, None] >= req_ends[None, :]).astype(jnp.int32), axis=1)
    request_hot = request[:, None] == jnp.arange(lengths.shape[0], dtype=jnp.int32)[None, :]
    adapter = jnp.sum(jnp.where(request_hot, request_adapter[None, :], 0), axis=1)
    adapter_count = adapter_down.shape[0] * n_row
    ranks = adapter_down.shape[0] * RANK
    down_rows = all_factors[:, :ranks].reshape(adapter_count * RANK, width_part)
    up_rows = all_factors[:, ranks:].reshape(adapter_count * RANK, width_part)
    rank_adapter = jnp.arange(adapter_count * RANK, dtype=jnp.int32) // RANK
    chosen = rank_adapter[:, None] == adapter[None, :]
    projected = lax.dot_general(
        down_rows, normed, (((1,), (1,)), ((), ())), preferred_element_type=jnp.float32
    )
    partial_low = jnp.sum(
        jnp.where(chosen, projected, 0.0).reshape(adapter_count, RANK, tok_rows), axis=0
    )
    assigned = routes.reshape(-1)
    assign_count = assigned.shape[0]
    expert_hot = (assigned[:, None] == jnp.arange(EXPERTS, dtype=jnp.int32)[None, :]).astype(
        jnp.int32
    )
    earlier = (
        jnp.arange(assign_count, dtype=jnp.int32)[:, None]
        > jnp.arange(assign_count, dtype=jnp.int32)[None, :]
    )
    before = jnp.dot(
        earlier.astype(jnp.bfloat16),
        expert_hot.astype(jnp.bfloat16),
        preferred_element_type=jnp.float32,
    ).astype(jnp.int32)
    slot_index = jnp.sum(before * expert_hot, axis=1)
    placed_at = assigned * SLOTS + slot_index
    placing = (jnp.arange(EXPERTS * SLOTS, dtype=jnp.int32)[:, None] == placed_at[None, :]).astype(
        jnp.bfloat16
    )
    placing_token = jnp.sum(placing.reshape(EXPERTS * SLOTS, tok_rows, TOPK), axis=2)
    buffer = jnp.dot(placing_token, normed, preferred_element_type=jnp.float32).astype(
        jnp.bfloat16
    )
    units = gate_weight.shape[1]
    pad_units = ((0, UNITS_PAD - units), (0, 0))
    weights = jnp.concatenate(
        [jnp.pad(gate_weight[0], pad_units), jnp.pad(up_weight[0], pad_units)], axis=0
    )
    down = jnp.pad(
        down_weight[0].reshape(n_col, units, width_part), ((0, 0),) + pad_units
    ).reshape(n_col * UNITS_PAD, width_part)
    returned, low_sum = main_exchange(
        buffer.reshape(EXPERTS, SLOTS, width_part), partial_low, weights, down.T, n_row, n_col
    )
    low_rank = low_sum.astype(jnp.bfloat16)
    expanded = jnp.where(
        chosen,
        jnp.broadcast_to(low_rank[None], (adapter_count, RANK, tok_rows)).reshape(
            adapter_count * RANK, tok_rows
        ),
        jnp.zeros((), jnp.bfloat16),
    )
    branch = lax.dot_general(
        expanded, up_rows, (((0,), (0,)), ((), ())), preferred_element_type=jnp.float32
    )
    twice = jnp.broadcast_to(
        placing.reshape(EXPERTS, 1, SLOTS, assign_count), (EXPERTS, 2, SLOTS, assign_count)
    ).reshape(EXPERTS * 2 * SLOTS, assign_count)
    gathered = lax.dot_general(
        twice,
        returned.reshape(EXPERTS * 2 * SLOTS, width_part),
        (((0,), (0,)), ((), ())),
        preferred_element_type=jnp.float32,
    )
    weighted = jnp.sum(
        gathered.reshape(tok_rows, TOPK, width_part) * route_weights[:, :, None], axis=1
    )
    return (weighted + branch).astype(jnp.bfloat16)


def solution(mesh):
    in_specs = (
        P("row", "col"),
        P("col"),
        P(),
        P(),
        P("row", None),
        P("row", None),
        P("row", "col", None),
        P("row", "col", None),
        P("row", None, "col"),
        P("row", "col", None),
        P("row", None, "col"),
    )
    out_specs = P("row", "col")
    return jax.shard_map(body, mesh=mesh, in_specs=in_specs, out_specs=out_specs, check_vma=False)
```

```python
import functools

import jax
import jax.numpy as jnp
from jax import lax
from jax.experimental import pallas as pl
from jax.experimental.pallas import tpu as pltpu
from jax.sharding import PartitionSpec as P

D = 2048
EXPERTS = 8
TOPK = 2
RANK = 16
CAP = 60
SLOTS = 64
RING = 4
UNITS_PAD = 96
MESH = pl.DeviceIdType.MESH
VMEM = pl.BlockSpec(memory_space=pltpu.VMEM)


def greet(peers):
    barrier = pltpu.get_barrier_semaphore()
    for row, col in peers:
        pl.semaphore_signal(barrier, inc=1, device_id=(row, col), device_id_type=MESH)
    pl.semaphore_wait(barrier, len(peers))


CHUNKS = 2


def main_kernel(
    n_row,
    buf_ref,
    scaled_ref,
    adapter_ref,
    sq_ref,
    gain_ref,
    ad_ref,
    w_ref,
    wd_ref,
    ret_ref,
    lowsum_ref,
    ad_all,
    toks,
    hid,
    wg,
    low,
    lowz,
    lowmid,
    lowx,
    gainz,
    gainx,
    osend,
    orecv,
    oacc,
    rbuf,
    send,
    local,
    d_sem,
    t_sem,
    p_sem,
    h_sem,
    lz_sem,
    lx_sem,
    gz_sem,
    gx_sem,
    a_sem,
    ap_sem,
    o_sem,
    r_sem,
):
    r, c = lax.axis_index("row"), lax.axis_index("col")
    core, half_row = r % 2, r // 2
    other = 1 - core
    partner = r + 1 - 2 * core
    zh, xx = c // RING, c % RING
    n_col = RING * RING
    pairs = n_row // 2
    rows_half = pairs * SLOTS
    chunk_rows = rows_half // CHUNKS
    piece = chunk_rows // 2
    width = buf_ref.shape[-1]

    def col_of(z, x):
        return (z % RING) * RING + x % RING

    z_right, z_left, z_far = col_of(zh + 1, xx), col_of(zh + 3, xx), col_of(zh + 2, xx)
    x_right, x_left, x_far = col_of(zh, xx + 1), col_of(zh, xx + 3), col_of(zh, xx + 2)
    row_steps = [(half_row + k) % pairs for k in range(1, pairs)]
    greet(
        [(2 * i + core, c) for i in row_steps]
        + [(r, p) for p in (z_right, z_left, z_far, x_right, x_left, x_far)]
        + [(partner, c)]
    )
    sends = []

    def push(src, dst, recv, row, col):
        copy = pltpu.make_async_remote_copy(
            src, dst, send.at[len(sends)], recv, (row, col), MESH
        )
        copy.start()
        sends.append(copy)

    def arrived(ref, recv):
        pltpu.make_async_copy(ref, ref, recv).wait()

    def expert_of(i):
        return (2 * i + core) // 4

    own = [
        pltpu.make_async_copy(
            buf_ref.at[expert_of(half_row)],
            toks.at[core, c, pl.ds(half_row * SLOTS, SLOTS)],
            local.at[0],
        ),
        pltpu.make_async_copy(ad_ref, ad_all.at[core, half_row], local.at[1]),
        pltpu.make_async_copy(gain_ref, gainz.at[zh], local.at[2]),
    ]
    for copy in own:
        copy.start()
    for i in row_steps:
        push(
            buf_ref.at[expert_of(i)],
            toks.at[core, c, pl.ds(half_row * SLOTS, SLOTS)],
            d_sem.at[half_row],
            2 * i + core,
            c,
        )
    for p in (z_right, z_left, z_far):
        push(gain_ref, gainz.at[zh], gz_sem.at[zh], r, p)
    for i in row_steps:
        push(ad_ref, ad_all.at[core, half_row], a_sem.at[half_row], 2 * i + core, c)
    for copy in own:
        copy.wait()
    for i in row_steps:
        arrived(toks.at[core, c, pl.ds(i * SLOTS, SLOTS)], d_sem.at[i])

    def gather(piece_of, sem, done):
        def go(col, part, to):
            push(piece_of(col, part), piece_of(col, part), sem.at[col * 2 + part], r, to)

        def got(col, part):
            arrived(piece_of(col, part), sem.at[col * 2 + part])

        def fan_x(col, part):
            go(col, part, x_right)
            go(col, part, x_left)

        def relay_x(z):
            from_left, from_right, far = col_of(z, xx + 3), col_of(z, xx + 1), col_of(z, xx + 2)
            got(from_left, 0)
            go(from_left, 0, x_right)
            got(from_right, 1)
            go(from_right, 1, x_left)
            got(from_left, 1)
            done(from_left)
            got(from_right, 0)
            done(from_right)
            return far

        def finish(far):
            got(far, 0)
            got(far, 1)
            done(far)

        def first():
            for part in range(2):
                go(c, part, z_right)
                go(c, part, z_left)
                fan_x(c, part)

        def rest(after_z):
            far_0 = relay_x(zh)
            got(z_left, 0)
            go(z_left, 0, z_right)
            fan_x(z_left, 0)
            got(z_right, 1)
            go(z_right, 1, z_left)
            fan_x(z_right, 1)
            after_z()
            got(z_left, 1)
            fan_x(z_left, 1)
            done(z_left)
            got(z_right, 0)
            fan_x(z_right, 0)
            done(z_right)
            finish(far_0)
            far_1 = relay_x(zh + 3)
            far_2 = relay_x(zh + 1)
            got(z_far, 0)
            fan_x(z_far, 0)
            got(z_far, 1)
            fan_x(z_far, 1)
            done(z_far)
            finish(far_1)
            finish(far_2)
            finish(relay_x(zh + 2))

        return first, rest

    def nothing(*unused):
        return None

    def token_gather(chunk):
        def rows(start, size):
            return pl.ds(chunk * chunk_rows + start, size)

        def share(col):
            ref = toks.at[core, col, rows(0, chunk_rows)]
            push(ref, ref, p_sem.at[chunk, col], partner, c)

        first, rest = gather(
            lambda col, part: toks.at[core, col, rows(part * piece, piece)],
            t_sem.at[chunk],
            share,
        )

        def start():
            first()
            share(c)

        return start, rest

    tok = [token_gather(chunk) for chunk in range(CHUNKS)]
    tok[0][0]()
    for k in range(1, RING):
        z = (zh + k) % RING
        arrived(gainz.at[z], gz_sem.at[z])
    keep = pltpu.make_async_copy(gainz, gainx.at[xx], local.at[3])
    keep.start()
    for p in (x_right, x_left, x_far):
        push(gainz, gainx.at[xx], gx_sem.at[xx], r, p)
    for i in row_steps:
        arrived(ad_all.at[core, i], a_sem.at[i])
    push(ad_all.at[core], ad_all.at[core], ap_sem.at[0], partner, c)
    arrived(ad_all.at[other], ap_sem.at[0])
    total = jnp.zeros((RANK, scaled_ref.shape[0]), jnp.float32)
    held = ad_ref.shape[0] // (2 * RANK)
    for parity in range(2):
        factors = ad_all[parity, :, : held * RANK, :].reshape(pairs * held * RANK, width)
        part = lax.dot_general(
            factors, scaled_ref[...], (((1,), (1,)), ((), ())), preferred_element_type=jnp.float32
        )
        at = lax.broadcasted_iota(jnp.int32, part.shape, 0) // RANK
        of = (2 * (at // held) + parity) * held + at % held
        part = jnp.where(of == adapter_ref[...], part, 0.0)
        total = total + jnp.sum(part.reshape(pairs * held, RANK, part.shape[1]), axis=0)
    low[pl.ds(0, RANK), :] = total
    low[pl.ds(RANK, 8), :] = sq_ref[...]
    for p in (z_right, z_left, z_far):
        push(low, lowz.at[zh], lz_sem.at[zh], r, p)
    tok[0][1](tok[1][0])
    total = low[...]
    for k in range(1, RING):
        z = (zh + k) % RING
        arrived(lowz.at[z], lz_sem.at[z])
        total = total + lowz[z]
    lowmid[...] = total
    for p in (x_right, x_left, x_far):
        push(lowmid, lowx.at[xx], lx_sem.at[xx], r, p)
    keep.wait()
    for k in range(1, RING):
        x = (xx + k) % RING
        arrived(gainx.at[x], gx_sem.at[x])
    for col in range(n_col):
        lanes = pl.ds(col * width, width)
        wg[:, lanes] = (
            w_ref[:, lanes].astype(jnp.float32) * gainx[col % RING, col // RING, 0:1, :]
        ).astype(jnp.bfloat16)

    step = 256
    steps = chunk_rows // step
    features = n_col * width
    ones = jnp.ones((8, width), jnp.float32)

    def hidden_of(chunk):
        for k in range(n_col):
            arrived(toks.at[other, k, pl.ds(chunk * chunk_rows, chunk_rows)], p_sem.at[chunk, k])

        def one(k, carry):
            parity = k // steps
            at = pl.multiple_of((k % steps) * step, step)
            from_row = pl.multiple_of(chunk * chunk_rows + at, step)
            pieces = [toks[parity, col, pl.ds(from_row, step), :] for col in range(n_col)]
            squares = jnp.zeros((step, width), jnp.float32)
            for x in pieces:
                wide = x.astype(jnp.float32)
                squares = squares + wide * wide
            mean = lax.dot_general(
                ones,
                squares,
                (((1,), (1,)), ((), ())),
                precision=lax.Precision.HIGHEST,
                preferred_element_type=jnp.float32,
            )[0:1]
            both = lax.dot_general(
                wg[...],
                jnp.concatenate(pieces, axis=1),
                (((1,), (1,)), ((), ())),
                preferred_element_type=jnp.float32,
            ) * lax.rsqrt(mean / features + 1e-06)
            gate, up = both[:UNITS_PAD], both[UNITS_PAD:]
            hid[chunk, parity, c, :, pl.ds(at, step)] = (
                gate / (1.0 + jnp.exp(-gate)) * up
            ).astype(jnp.bfloat16)
            return carry

        lax.fori_loop(0, 2 * steps, one, 0)

    def hidden_gather(chunk):
        return gather(lambda col, part: hid.at[chunk, part, col], h_sem.at[chunk], nothing)

    def out_of(chunk):
        def one(parity, into, k, carry):
            at = pl.multiple_of(k * step, step)
            h = hid[chunk, parity, :, :, pl.ds(at, step)].reshape(n_col * UNITS_PAD, step)
            y = jnp.dot(wd_ref[...], h, preferred_element_type=jnp.float32)
            into[chunk, pl.ds(at, step), :] = jnp.transpose(y).astype(into.dtype)
            return carry

        lax.fori_loop(0, steps, functools.partial(one, other, osend), 0)
        push(osend.at[chunk], orecv.at[chunk], o_sem.at[chunk], partner, c)
        lax.fori_loop(0, steps, functools.partial(one, core, oacc), 0)

    def total_of(chunk):
        arrived(orecv.at[chunk], o_sem.at[chunk])
        rbuf[chunk] = (oacc[chunk] + orecv[chunk].astype(jnp.float32)).astype(jnp.bfloat16)

    hids = [hidden_gather(chunk) for chunk in range(CHUNKS)]
    hidden_of(0)
    hids[0][0]()
    tok[1][1](nothing)
    hidden_of(1)
    hids[0][1](hids[1][0])
    for k in range(1, RING):
        x = (xx + k) % RING
        arrived(lowx.at[x], lx_sem.at[x])
        total = total + lowx[x]
    lowsum_ref[...] = total
    out_of(0)
    hids[1][1](nothing)
    total_of(0)
    out_of(1)
    total_of(1)
    per = pairs // CHUNKS

    def sums_of(i):
        return rbuf.at[i // per, pl.ds((i % per) * SLOTS, SLOTS)]

    back = pltpu.make_async_copy(sums_of(half_row), ret_ref.at[half_row], local.at[0])
    back.start()
    for i in row_steps:
        push(sums_of(i), ret_ref.at[half_row], r_sem.at[half_row], 2 * i + core, c)
    back.wait()
    for i in row_steps:
        arrived(ret_ref.at[i], r_sem.at[i])
    for copy in sends:
        copy.wait_send()


def main_exchange(buffer, scaled, adapter, squares, gain, factors, weights, down, n_row, n_col):
    pairs = n_row // 2
    rows_half = pairs * SLOTS
    chunk_rows = rows_half // CHUNKS
    width = buffer.shape[-1]
    low_shape = (RANK + 8, scaled.shape[0])
    dma = pltpu.SemaphoreType.DMA
    sends = 3 * (pairs - 1) + 1 + 12 + CHUNKS * (60 + n_col + 1)
    return pl.pallas_call(
        functools.partial(main_kernel, n_row),
        out_shape=(
            jax.ShapeDtypeStruct((pairs, SLOTS, width), jnp.bfloat16),
            jax.ShapeDtypeStruct(low_shape, jnp.float32),
            jax.ShapeDtypeStruct((2, pairs) + factors.shape, jnp.bfloat16),
        ),
        in_specs=[VMEM] * 8,
        out_specs=(VMEM,) * 3,
        scratch_shapes=[
            pltpu.VMEM((2, n_col, rows_half, width), jnp.bfloat16),
            pltpu.VMEM((CHUNKS, 2, n_col, UNITS_PAD, chunk_rows), jnp.bfloat16),
            pltpu.VMEM(weights.shape, jnp.bfloat16),
            pltpu.VMEM(low_shape, jnp.float32),
            pltpu.VMEM((RING,) + low_shape, jnp.float32),
            pltpu.VMEM(low_shape, jnp.float32),
            pltpu.VMEM((RING,) + low_shape, jnp.float32),
            pltpu.VMEM((RING,) + gain.shape, jnp.float32),
            pltpu.VMEM((RING, RING) + gain.shape, jnp.float32),
            pltpu.VMEM((CHUNKS, chunk_rows, width), jnp.bfloat16),
            pltpu.VMEM((CHUNKS, chunk_rows, width), jnp.bfloat16),
            pltpu.VMEM((CHUNKS, chunk_rows, width), jnp.float32),
            pltpu.VMEM((CHUNKS, chunk_rows, width), jnp.bfloat16),
            dma((sends,)),
            dma((4,)),
            dma((pairs,)),
            dma((CHUNKS, 2 * n_col)),
            dma((CHUNKS, n_col)),
            dma((CHUNKS, 2 * n_col)),
            dma((RING,)),
            dma((RING,)),
            dma((RING,)),
            dma((RING,)),
            dma((pairs,)),
            dma((1,)),
            dma((CHUNKS,)),
            dma((pairs,)),
        ],
        compiler_params=pltpu.CompilerParams(collective_id=1, has_side_effects=True),
    )(buffer, scaled, adapter, squares, gain, factors, weights, down)


def body(
    tokens,
    norm_gain,
    lengths,
    request_adapter,
    routes,
    route_weights,
    gate_weight,
    up_weight,
    down_weight,
    adapter_down,
    adapter_up,
):
    tok_rows, width_part = tokens.shape
    n_row, n_col = lax.axis_size("row"), lax.axis_size("col")
    widened = tokens.astype(jnp.float32)
    own_squares = jnp.sum(widened * widened, axis=1)[None, :]
    own_factors = jnp.concatenate(
        [
            jnp.transpose(adapter_down, (0, 2, 1)).reshape(-1, width_part),
            adapter_up.reshape(-1, width_part),
        ],
        axis=0,
    )
    scaled = (widened * norm_gain[None, :]).astype(jnp.bfloat16)
    req_ends = jnp.cumsum(lengths)
    position = lax.axis_index("row") * tok_rows + jnp.arange(tok_rows, dtype=jnp.int32)
    request = jnp.sum((position[:, None] >= req_ends[None, :]).astype(jnp.int32), axis=1)
    request_hot = request[:, None] == jnp.arange(lengths.shape[0], dtype=jnp.int32)[None, :]
    adapter = jnp.sum(jnp.where(request_hot, request_adapter[None, :], 0), axis=1)
    adapter_count = adapter_down.shape[0] * n_row
    ranks = adapter_down.shape[0] * RANK
    rank_adapter = jnp.arange(adapter_count * RANK, dtype=jnp.int32) // RANK
    chosen = rank_adapter[:, None] == adapter[None, :]
    assigned = routes.reshape(-1)
    assign_count = assigned.shape[0]
    expert_hot = (assigned[:, None] == jnp.arange(EXPERTS, dtype=jnp.int32)[None, :]).astype(
        jnp.int32
    )
    earlier = (
        jnp.arange(assign_count, dtype=jnp.int32)[:, None]
        > jnp.arange(assign_count, dtype=jnp.int32)[None, :]
    )
    before = jnp.dot(
        earlier.astype(jnp.bfloat16),
        expert_hot.astype(jnp.bfloat16),
        preferred_element_type=jnp.float32,
    ).astype(jnp.int32)
    slot_index = jnp.sum(before * expert_hot, axis=1)
    placed_at = assigned * SLOTS + slot_index
    placing = (jnp.arange(EXPERTS * SLOTS, dtype=jnp.int32)[:, None] == placed_at[None, :]).astype(
        jnp.bfloat16
    )
    placing_token = jnp.sum(placing.reshape(EXPERTS * SLOTS, tok_rows, TOPK), axis=2)
    buffer = jnp.dot(placing_token, tokens, preferred_element_type=jnp.float32).astype(
        jnp.bfloat16
    )
    units = gate_weight.shape[1]
    pad_units = ((0, UNITS_PAD - units), (0, 0))
    weights = jnp.concatenate(
        [jnp.pad(gate_weight[0], pad_units), jnp.pad(up_weight[0], pad_units)], axis=0
    )
    down = jnp.pad(
        down_weight[0].reshape(n_col, units, width_part), ((0, 0),) + pad_units
    ).reshape(n_col * UNITS_PAD, width_part)
    returned, low_sum, factors = main_exchange(
        buffer.reshape(EXPERTS, SLOTS, width_part),
        scaled,
        adapter[None, :],
        jnp.broadcast_to(own_squares, (8, tok_rows)),
        jnp.broadcast_to(norm_gain[None, :], (8, width_part)),
        own_factors,
        weights,
        down.T,
        n_row,
        n_col,
    )
    scale = lax.rsqrt(low_sum[RANK] / D + 1e-06)
    low_rank = (low_sum[:RANK] * scale[None, :]).astype(jnp.bfloat16)
    up_rows = jnp.transpose(factors[:, :, ranks:], (1, 0, 2, 3)).reshape(
        adapter_count * RANK, width_part
    )
    expanded = jnp.where(
        chosen,
        jnp.broadcast_to(low_rank[None], (adapter_count, RANK, tok_rows)).reshape(
            adapter_count * RANK, tok_rows
        ),
        jnp.zeros((), jnp.bfloat16),
    )
    branch = lax.dot_general(
        expanded, up_rows, (((0,), (0,)), ((), ())), preferred_element_type=jnp.float32
    )
    twice = jnp.broadcast_to(
        placing.reshape(EXPERTS, 1, SLOTS, assign_count), (EXPERTS, 2, SLOTS, assign_count)
    ).reshape(EXPERTS * 2 * SLOTS, assign_count)
    gathered = lax.dot_general(
        twice,
        returned.reshape(EXPERTS * 2 * SLOTS, width_part),
        (((0,), (0,)), ((), ())),
        preferred_element_type=jnp.float32,
    )
    weighted = jnp.sum(
        gathered.reshape(tok_rows, TOPK, width_part) * route_weights[:, :, None], axis=1
    )
    return (weighted + branch).astype(jnp.bfloat16)


def solution(mesh):
    in_specs = (
        P("row", "col"),
        P("col"),
        P(),
        P(),
        P("row", None),
        P("row", None),
        P("row", "col", None),
        P("row", "col", None),
        P("row", None, "col"),
        P("row", "col", None),
        P("row", None, "col"),
    )
    out_specs = P("row", "col")
    return jax.shard_map(body, mesh=mesh, in_specs=in_specs, out_specs=out_specs, check_vma=False)
```

```python
import functools

import jax
import jax.numpy as jnp
from jax import lax
from jax.experimental import pallas as pl
from jax.experimental.pallas import tpu as pltpu
from jax.sharding import PartitionSpec as P

D = 2048
EXPERTS = 8
TOPK = 2
RANK = 16
CAP = 60
SLOTS = 64
RING = 4
UNITS_PAD = 96
MESH = pl.DeviceIdType.MESH
VMEM = pl.BlockSpec(memory_space=pltpu.VMEM)


def greet(peers):
    barrier = pltpu.get_barrier_semaphore()
    for row, col in peers:
        pl.semaphore_signal(barrier, inc=1, device_id=(row, col), device_id_type=MESH)
    pl.semaphore_wait(barrier, len(peers))


CHUNKS = 2


def main_kernel(
    n_row,
    buf_ref,
    tok_ref,
    adapter_ref,
    gain_ref,
    first_ref,
    second_ref,
    gate_ref,
    up_ref,
    down_ref,
    ret_ref,
    lowsum_ref,
    ad_all,
    toks,
    hid,
    wg,
    wd,
    ad_own,
    low,
    lowz,
    lowmid,
    lowx,
    gainz,
    gainx,
    osend,
    orecv,
    both_out,
    rbuf,
    send,
    local,
    d_sem,
    t_sem,
    p_sem,
    h_sem,
    lz_sem,
    lx_sem,
    gz_sem,
    gx_sem,
    a_sem,
    ap_sem,
    o_sem,
    r_sem,
):
    r, c = lax.axis_index("row"), lax.axis_index("col")
    core, half_row = r % 2, r // 2
    other = 1 - core
    partner = r + 1 - 2 * core
    zh, xx = c // RING, c % RING
    n_col = RING * RING
    pairs = n_row // 2
    rows_half = pairs * SLOTS
    chunk_rows = rows_half // CHUNKS
    piece = chunk_rows // 2
    width = buf_ref.shape[-1]

    def col_of(z, x):
        return (z % RING) * RING + x % RING

    z_right, z_left, z_far = col_of(zh + 1, xx), col_of(zh + 3, xx), col_of(zh + 2, xx)
    x_right, x_left, x_far = col_of(zh, xx + 1), col_of(zh, xx + 3), col_of(zh, xx + 2)
    row_steps = [(half_row + k) % pairs for k in range(1, pairs)]
    greet(
        [(2 * i + core, c) for i in row_steps]
        + [(r, p) for p in (z_right, z_left, z_far, x_right, x_left, x_far)]
        + [(partner, c)]
    )
    sends = []

    def push(src, dst, recv, row, col):
        copy = pltpu.make_async_remote_copy(
            src, dst, send.at[len(sends)], recv, (row, col), MESH
        )
        copy.start()
        sends.append(copy)

    def arrived(ref, recv):
        pltpu.make_async_copy(ref, ref, recv).wait()

    def expert_of(i):
        return (2 * i + core) // 4

    own = [
        pltpu.make_async_copy(
            buf_ref.at[expert_of(half_row)],
            toks.at[core, c, pl.ds(half_row * SLOTS, SLOTS)],
            local.at[0],
        ),
        pltpu.make_async_copy(gain_ref, gainz.at[zh], local.at[2]),
    ]
    for copy in own:
        copy.start()
    for i in row_steps:
        push(
            buf_ref.at[expert_of(i)],
            toks.at[core, c, pl.ds(half_row * SLOTS, SLOTS)],
            d_sem.at[half_row],
            2 * i + core,
            c,
        )
    for p in (z_right, z_left, z_far):
        push(gain_ref, gainz.at[zh], gz_sem.at[zh], r, p)
    held = first_ref.shape[0]
    unit_matrix = (
        lax.broadcasted_iota(jnp.int32, (RANK, RANK), 0)
        == lax.broadcasted_iota(jnp.int32, (RANK, RANK), 1)
    ).astype(jnp.bfloat16)
    for a in range(held):
        ad_own[pl.ds(a * RANK, RANK), :] = lax.dot_general(
            unit_matrix,
            first_ref[a],
            (((1,), (1,)), ((), ())),
            preferred_element_type=jnp.float32,
        ).astype(jnp.bfloat16)
        ad_own[pl.ds((held + a) * RANK, RANK), :] = second_ref[a]
    keep_own = pltpu.make_async_copy(ad_own, ad_all.at[core, half_row], local.at[1])
    keep_own.start()
    for i in row_steps:
        push(ad_own, ad_all.at[core, half_row], a_sem.at[half_row], 2 * i + core, c)
    for copy in own:
        copy.wait()
    for i in row_steps:
        arrived(toks.at[core, c, pl.ds(i * SLOTS, SLOTS)], d_sem.at[i])

    def gather(piece_of, sem, done):
        def go(col, part, to):
            push(piece_of(col, part), piece_of(col, part), sem.at[col * 2 + part], r, to)

        def got(col, part):
            arrived(piece_of(col, part), sem.at[col * 2 + part])

        def fan_x(col, part):
            go(col, part, x_right)
            go(col, part, x_left)

        def relay_x(z):
            from_left, from_right, far = col_of(z, xx + 3), col_of(z, xx + 1), col_of(z, xx + 2)
            got(from_left, 0)
            go(from_left, 0, x_right)
            got(from_right, 1)
            go(from_right, 1, x_left)
            got(from_left, 1)
            done(from_left)
            got(from_right, 0)
            done(from_right)
            return far

        def finish(far):
            got(far, 0)
            got(far, 1)
            done(far)

        def first():
            for part in range(2):
                go(c, part, z_right)
                go(c, part, z_left)
                fan_x(c, part)

        def rest(after_z):
            far_0 = relay_x(zh)
            got(z_left, 0)
            go(z_left, 0, z_right)
            fan_x(z_left, 0)
            got(z_right, 1)
            go(z_right, 1, z_left)
            fan_x(z_right, 1)
            after_z()
            got(z_left, 1)
            fan_x(z_left, 1)
            done(z_left)
            got(z_right, 0)
            fan_x(z_right, 0)
            done(z_right)
            finish(far_0)
            far_1 = relay_x(zh + 3)
            far_2 = relay_x(zh + 1)
            got(z_far, 0)
            fan_x(z_far, 0)
            got(z_far, 1)
            fan_x(z_far, 1)
            done(z_far)
            finish(far_1)
            finish(far_2)
            finish(relay_x(zh + 2))

        return first, rest

    def nothing(*unused):
        return None

    def token_gather(chunk):
        def rows(start, size):
            return pl.ds(chunk * chunk_rows + start, size)

        def share(col):
            ref = toks.at[core, col, rows(0, chunk_rows)]
            push(ref, ref, p_sem.at[chunk, col], partner, c)

        first, rest = gather(
            lambda col, part: toks.at[core, col, rows(part * piece, piece)],
            t_sem.at[chunk],
            share,
        )

        def start():
            first()
            share(c)

        return start, rest

    tok = [token_gather(chunk) for chunk in range(CHUNKS)]
    for start, _ in tok:
        start()
    units = gate_ref.shape[0]
    rows = down_ref[...].astype(jnp.float32)
    blank = jnp.zeros((units, width), jnp.float32)
    for parity in range(2):
        spread = []
        for col in range(n_col):
            mine = rows[col * units : (col + 1) * units]
            spread += [mine, blank] if parity == 0 else [blank, mine]
        wd[pl.ds(parity * width, width), :] = jnp.transpose(
            jnp.concatenate(spread, axis=0)
        ).astype(jnp.bfloat16)
    for k in range(1, RING):
        z = (zh + k) % RING
        arrived(gainz.at[z], gz_sem.at[z])
    keep = pltpu.make_async_copy(gainz, gainx.at[xx], local.at[3])
    keep.start()
    for p in (x_right, x_left, x_far):
        push(gainz, gainx.at[xx], gx_sem.at[xx], r, p)
    for i in row_steps:
        arrived(ad_all.at[core, i], a_sem.at[i])
    keep_own.wait()
    push(ad_all.at[core], ad_all.at[core], ap_sem.at[0], partner, c)
    arrived(ad_all.at[other], ap_sem.at[0])
    wide = tok_ref[...].astype(jnp.float32)
    scaled = (wide * gain_ref[...]).astype(jnp.bfloat16)
    ones = jnp.ones((8, width), jnp.float32)
    total = jnp.zeros((RANK, tok_ref.shape[0]), jnp.float32)
    for parity in range(2):
        factors = ad_all[parity, :, : held * RANK, :].reshape(pairs * held * RANK, width)
        part = lax.dot_general(
            factors, scaled, (((1,), (1,)), ((), ())), preferred_element_type=jnp.float32
        )
        at = lax.broadcasted_iota(jnp.int32, part.shape, 0) // RANK
        of = (2 * (at // held) + parity) * held + at % held
        part = jnp.where(of == adapter_ref[...], part, 0.0)
        total = total + jnp.sum(part.reshape(pairs * held, RANK, part.shape[1]), axis=0)
    low[pl.ds(0, RANK), :] = total
    low[pl.ds(RANK, 8), :] = lax.dot_general(
        ones,
        wide * wide,
        (((1,), (1,)), ((), ())),
        precision=lax.Precision.HIGHEST,
        preferred_element_type=jnp.float32,
    )
    for p in (z_right, z_left, z_far):
        push(low, lowz.at[zh], lz_sem.at[zh], r, p)
    tok[0][1](nothing)
    total = low[...]
    for k in range(1, RING):
        z = (zh + k) % RING
        arrived(lowz.at[z], lz_sem.at[z])
        total = total + lowz[z]
    lowmid[...] = total
    for p in (x_right, x_left, x_far):
        push(lowmid, lowx.at[xx], lx_sem.at[xx], r, p)
    keep.wait()
    for k in range(1, RING):
        x = (xx + k) % RING
        arrived(gainx.at[x], gx_sem.at[x])
    nil = jnp.zeros((UNITS_PAD - units, width), jnp.float32)
    for col in range(n_col):
        lanes = pl.ds(col * width, width)
        gain = gainx[col % RING, col // RING]
        wg[:, lanes] = jnp.concatenate(
            [
                gate_ref[:, lanes].astype(jnp.float32) * gain,
                nil,
                up_ref[:, lanes].astype(jnp.float32) * gain,
                nil,
            ],
            axis=0,
        ).astype(jnp.bfloat16)

    step = 256
    steps = chunk_rows // step
    features = n_col * width

    def hidden_of(chunk):
        for k in range(n_col):
            arrived(toks.at[other, k, pl.ds(chunk * chunk_rows, chunk_rows)], p_sem.at[chunk, k])

        def of_parity(parity, at):
            from_row = pl.multiple_of(chunk * chunk_rows + at, step)
            pieces = [toks[parity, col, pl.ds(from_row, step), :] for col in range(n_col)]
            squares = jnp.zeros((step, width), jnp.float32)
            for x in pieces:
                wide = x.astype(jnp.float32)
                squares = squares + wide * wide
            mean = lax.dot_general(
                ones,
                squares,
                (((1,), (1,)), ((), ())),
                precision=lax.Precision.HIGHEST,
                preferred_element_type=jnp.float32,
            )[0:1]
            both = lax.dot_general(
                wg[...],
                jnp.concatenate(pieces, axis=1),
                (((1,), (1,)), ((), ())),
                preferred_element_type=jnp.float32,
            ) * lax.rsqrt(mean / features + 1e-06)
            gate, up = both[:units], both[UNITS_PAD : UNITS_PAD + units]
            return gate / (1.0 + jnp.exp(-gate)) * up

        def one(k, carry):
            at = pl.multiple_of(k * step, step)
            hid[chunk, c, :, pl.ds(at, step)] = jnp.concatenate(
                [of_parity(0, at), of_parity(1, at)], axis=0
            ).astype(jnp.bfloat16)
            return carry

        lax.fori_loop(0, steps, one, 0)

    def hidden_gather(chunk):
        def piece_of(col, part):
            half = chunk_rows // 2
            return hid.at[chunk, col, :, pl.ds(part * half, half)]

        return gather(piece_of, h_sem.at[chunk], nothing)

    def out_of(chunk):
        def one(k, carry):
            at = pl.multiple_of(k * step, step)
            h = hid[chunk, :, :, pl.ds(at, step)].reshape(n_col * 2 * units, step)
            y = jnp.dot(wd[...], h, preferred_element_type=jnp.float32)
            for parity in range(2):
                both_out[chunk, parity, pl.ds(at, step), :] = jnp.transpose(
                    y[parity * width : (parity + 1) * width]
                )
            return carry

        lax.fori_loop(0, steps, one, 0)
        osend[chunk] = both_out[chunk, other].astype(jnp.bfloat16)
        push(osend.at[chunk], orecv.at[chunk], o_sem.at[chunk], partner, c)

    def total_of(chunk):
        arrived(orecv.at[chunk], o_sem.at[chunk])
        rbuf[chunk] = (both_out[chunk, core] + orecv[chunk].astype(jnp.float32)).astype(jnp.bfloat16)

    hids = [hidden_gather(chunk) for chunk in range(CHUNKS)]
    hidden_of(0)
    hids[0][0]()
    tok[1][1](nothing)
    hidden_of(1)
    hids[1][0]()
    hids[0][1](nothing)
    for k in range(1, RING):
        x = (xx + k) % RING
        arrived(lowx.at[x], lx_sem.at[x])
        total = total + lowx[x]
    lowsum_ref[...] = total
    out_of(0)
    hids[1][1](nothing)
    total_of(0)
    out_of(1)
    total_of(1)
    per = pairs // CHUNKS

    def sums_of(i):
        return rbuf.at[i // per, pl.ds((i % per) * SLOTS, SLOTS)]

    back = pltpu.make_async_copy(sums_of(half_row), ret_ref.at[half_row], local.at[0])
    back.start()
    for i in row_steps:
        push(sums_of(i), ret_ref.at[half_row], r_sem.at[half_row], 2 * i + core, c)
    back.wait()
    for i in row_steps:
        arrived(ret_ref.at[i], r_sem.at[i])
    for copy in sends:
        copy.wait_send()


def main_exchange(
    buffer, tokens, adapter, gain, first, second, gate_rows, up_rows, down_rows, n_row, n_col
):
    pairs = n_row // 2
    rows_half = pairs * SLOTS
    chunk_rows = rows_half // CHUNKS
    width = buffer.shape[-1]
    low_shape = (RANK + 8, tokens.shape[0])
    units = gate_rows.shape[0]
    factors_shape = (2 * RANK * first.shape[0], width)
    dma = pltpu.SemaphoreType.DMA
    sends = 3 * (pairs - 1) + 1 + 12 + CHUNKS * (60 + n_col + 1)
    return pl.pallas_call(
        functools.partial(main_kernel, n_row),
        out_shape=(
            jax.ShapeDtypeStruct((pairs, SLOTS, width), jnp.bfloat16),
            jax.ShapeDtypeStruct(low_shape, jnp.float32),
            jax.ShapeDtypeStruct((2, pairs) + factors_shape, jnp.bfloat16),
        ),
        in_specs=[VMEM] * 9,
        out_specs=(VMEM,) * 3,
        scratch_shapes=[
            pltpu.VMEM((2, n_col, rows_half, width), jnp.bfloat16),
            pltpu.VMEM((CHUNKS, n_col, 2 * units, chunk_rows), jnp.bfloat16),
            pltpu.VMEM((2 * UNITS_PAD, n_col * width), jnp.bfloat16),
            pltpu.VMEM((2 * width, n_col * 2 * units), jnp.bfloat16),
            pltpu.VMEM(factors_shape, jnp.bfloat16),
            pltpu.VMEM(low_shape, jnp.float32),
            pltpu.VMEM((RING,) + low_shape, jnp.float32),
            pltpu.VMEM(low_shape, jnp.float32),
            pltpu.VMEM((RING,) + low_shape, jnp.float32),
            pltpu.VMEM((RING,) + gain.shape, jnp.float32),
            pltpu.VMEM((RING, RING) + gain.shape, jnp.float32),
            pltpu.VMEM((CHUNKS, chunk_rows, width), jnp.bfloat16),
            pltpu.VMEM((CHUNKS, chunk_rows, width), jnp.bfloat16),
            pltpu.VMEM((CHUNKS, 2, chunk_rows, width), jnp.float32),
            pltpu.VMEM((CHUNKS, chunk_rows, width), jnp.bfloat16),
            dma((sends,)),
            dma((4,)),
            dma((pairs,)),
            dma((CHUNKS, 2 * n_col)),
            dma((CHUNKS, n_col)),
            dma((CHUNKS, 2 * n_col)),
            dma((RING,)),
            dma((RING,)),
            dma((RING,)),
            dma((RING,)),
            dma((pairs,)),
            dma((1,)),
            dma((CHUNKS,)),
            dma((pairs,)),
        ],
        compiler_params=pltpu.CompilerParams(collective_id=1, has_side_effects=True),
    )(buffer, tokens, adapter, gain, first, second, gate_rows, up_rows, down_rows)


def body(
    tokens,
    norm_gain,
    lengths,
    request_adapter,
    routes,
    route_weights,
    gate_weight,
    up_weight,
    down_weight,
    adapter_down,
    adapter_up,
):
    tok_rows, width_part = tokens.shape
    n_row, n_col = lax.axis_size("row"), lax.axis_size("col")
    req_ends = jnp.cumsum(lengths)
    position = lax.axis_index("row") * tok_rows + jnp.arange(tok_rows, dtype=jnp.int32)
    request = jnp.sum((position[:, None] >= req_ends[None, :]).astype(jnp.int32), axis=1)
    request_hot = request[:, None] == jnp.arange(lengths.shape[0], dtype=jnp.int32)[None, :]
    adapter = jnp.sum(jnp.where(request_hot, request_adapter[None, :], 0), axis=1)
    adapter_count = adapter_down.shape[0] * n_row
    ranks = adapter_down.shape[0] * RANK
    rank_adapter = jnp.arange(adapter_count * RANK, dtype=jnp.int32) // RANK
    chosen = rank_adapter[:, None] == adapter[None, :]
    assigned = routes.reshape(-1)
    assign_count = assigned.shape[0]
    expert_hot = (assigned[:, None] == jnp.arange(EXPERTS, dtype=jnp.int32)[None, :]).astype(
        jnp.int32
    )
    earlier = (
        jnp.arange(assign_count, dtype=jnp.int32)[:, None]
        > jnp.arange(assign_count, dtype=jnp.int32)[None, :]
    )
    before = jnp.dot(
        earlier.astype(jnp.bfloat16),
        expert_hot.astype(jnp.bfloat16),
        preferred_element_type=jnp.float32,
    ).astype(jnp.int32)
    slot_index = jnp.sum(before * expert_hot, axis=1)
    placed_at = assigned * SLOTS + slot_index
    placing = (jnp.arange(EXPERTS * SLOTS, dtype=jnp.int32)[:, None] == placed_at[None, :]).astype(
        jnp.bfloat16
    )
    placing_token = jnp.sum(placing.reshape(EXPERTS * SLOTS, tok_rows, TOPK), axis=2)
    buffer = jnp.dot(placing_token, tokens, preferred_element_type=jnp.float32).astype(
        jnp.bfloat16
    )
    returned, low_sum, factors = main_exchange(
        buffer.reshape(EXPERTS, SLOTS, width_part),
        tokens,
        adapter[None, :],
        norm_gain[None, :],
        adapter_down,
        adapter_up,
        gate_weight[0],
        up_weight[0],
        down_weight[0],
        n_row,
        n_col,
    )
    scale = lax.rsqrt(low_sum[RANK] / D + 1e-06)
    low_rank = (low_sum[:RANK] * scale[None, :]).astype(jnp.bfloat16)
    up_rows = jnp.transpose(factors[:, :, ranks:], (1, 0, 2, 3)).reshape(
        adapter_count * RANK, width_part
    )
    expanded = jnp.where(
        chosen,
        jnp.broadcast_to(low_rank[None], (adapter_count, RANK, tok_rows)).reshape(
            adapter_count * RANK, tok_rows
        ),
        jnp.zeros((), jnp.bfloat16),
    )
    branch = lax.dot_general(
        expanded, up_rows, (((0,), (0,)), ((), ())), preferred_element_type=jnp.float32
    )
    twice = jnp.broadcast_to(
        placing.reshape(EXPERTS, 1, SLOTS, assign_count), (EXPERTS, 2, SLOTS, assign_count)
    ).reshape(EXPERTS * 2 * SLOTS, assign_count)
    gathered = lax.dot_general(
        twice,
        returned.reshape(EXPERTS * 2 * SLOTS, width_part),
        (((0,), (0,)), ((), ())),
        preferred_element_type=jnp.float32,
    )
    weighted = jnp.sum(
        gathered.reshape(tok_rows, TOPK, width_part) * route_weights[:, :, None], axis=1
    )
    return (weighted + branch).astype(jnp.bfloat16)


def solution(mesh):
    in_specs = (
        P("row", "col"),
        P("col"),
        P(),
        P(),
        P("row", None),
        P("row", None),
        P("row", "col", None),
        P("row", "col", None),
        P("row", None, "col"),
        P("row", "col", None),
        P("row", None, "col"),
    )
    out_specs = P("row", "col")
    return jax.shard_map(body, mesh=mesh, in_specs=in_specs, out_specs=out_specs, check_vma=False)
```

```python
import functools

import jax
import jax.numpy as jnp
from jax import lax
from jax.experimental import pallas as pl
from jax.experimental.pallas import tpu as pltpu
from jax.sharding import PartitionSpec as P

D = 2048
EXPERTS = 8
TOPK = 2
RANK = 16
CAP = 60
SLOTS = 64
RING = 4
UNITS_PAD = 96
MESH = pl.DeviceIdType.MESH
VMEM = pl.BlockSpec(memory_space=pltpu.VMEM)


def greet(peers):
    barrier = pltpu.get_barrier_semaphore()
    for row, col in peers:
        pl.semaphore_signal(barrier, inc=1, device_id=(row, col), device_id_type=MESH)
    pl.semaphore_wait(barrier, len(peers))


CHUNKS = 2


def main_kernel(
    n_row,
    buf_ref,
    tok_ref,
    adapter_ref,
    gain_ref,
    first_ref,
    second_ref,
    gate_ref,
    up_ref,
    down_ref,
    ret_ref,
    lowsum_ref,
    ad_all,
    toks,
    hid,
    wg,
    wd,
    ad_own,
    low,
    lowz,
    lowmid,
    lowx,
    gainz,
    gainx,
    osend,
    orecv,
    both_out,
    rbuf,
    send,
    local,
    d_sem,
    t_sem,
    p_sem,
    h_sem,
    lz_sem,
    lx_sem,
    gz_sem,
    gx_sem,
    a_sem,
    ap_sem,
    o_sem,
    r_sem,
):
    r, c = lax.axis_index("row"), lax.axis_index("col")
    core, half_row = r % 2, r // 2
    other = 1 - core
    partner = r + 1 - 2 * core
    zh, xx = c // RING, c % RING
    n_col = RING * RING
    pairs = n_row // 2
    rows_half = pairs * SLOTS
    chunk_rows = rows_half // CHUNKS
    piece = chunk_rows // 2
    width = buf_ref.shape[-1]

    def col_of(z, x):
        return (z % RING) * RING + x % RING

    z_right, z_left, z_far = col_of(zh + 1, xx), col_of(zh + 3, xx), col_of(zh + 2, xx)
    x_right, x_left, x_far = col_of(zh, xx + 1), col_of(zh, xx + 3), col_of(zh, xx + 2)
    row_steps = [(half_row + k) % pairs for k in range(1, pairs)]
    greet(
        [(2 * i + core, c) for i in row_steps]
        + [(r, p) for p in (z_right, z_left, z_far, x_right, x_left, x_far)]
        + [(partner, c)]
    )
    sends = []

    def push(src, dst, recv, row, col):
        copy = pltpu.make_async_remote_copy(
            src, dst, send.at[len(sends)], recv, (row, col), MESH
        )
        copy.start()
        sends.append(copy)

    def arrived(ref, recv):
        pltpu.make_async_copy(ref, ref, recv).wait()

    def expert_of(i):
        return (2 * i + core) // 4

    own = [
        pltpu.make_async_copy(
            buf_ref.at[expert_of(half_row)],
            toks.at[core, c, pl.ds(half_row * SLOTS, SLOTS)],
            local.at[0],
        ),
        pltpu.make_async_copy(gain_ref, gainz.at[zh], local.at[2]),
    ]
    for copy in own:
        copy.start()
    for i in row_steps:
        push(
            buf_ref.at[expert_of(i)],
            toks.at[core, c, pl.ds(half_row * SLOTS, SLOTS)],
            d_sem.at[half_row],
            2 * i + core,
            c,
        )
    for p in (z_right, z_left, z_far):
        push(gain_ref, gainz.at[zh], gz_sem.at[zh], r, p)
    for copy in own:
        copy.wait()
    for i in row_steps:
        arrived(toks.at[core, c, pl.ds(i * SLOTS, SLOTS)], d_sem.at[i])

    def gather(piece_of, sem, done):
        def go(col, part, to):
            push(piece_of(col, part), piece_of(col, part), sem.at[col * 2 + part], r, to)

        def got(col, part):
            arrived(piece_of(col, part), sem.at[col * 2 + part])

        def fan_x(col, part):
            go(col, part, x_right)
            go(col, part, x_left)

        def relay_x(z):
            from_left, from_right, far = col_of(z, xx + 3), col_of(z, xx + 1), col_of(z, xx + 2)
            got(from_left, 0)
            go(from_left, 0, x_right)
            got(from_right, 1)
            go(from_right, 1, x_left)
            got(from_left, 1)
            done(from_left)
            got(from_right, 0)
            done(from_right)
            return far

        def finish(far):
            got(far, 0)
            got(far, 1)
            done(far)

        def first():
            for part in range(2):
                go(c, part, z_right)
                go(c, part, z_left)
                fan_x(c, part)

        def rest(after_z):
            far_0 = relay_x(zh)
            got(z_left, 0)
            go(z_left, 0, z_right)
            fan_x(z_left, 0)
            got(z_right, 1)
            go(z_right, 1, z_left)
            fan_x(z_right, 1)
            after_z()
            got(z_left, 1)
            fan_x(z_left, 1)
            done(z_left)
            got(z_right, 0)
            fan_x(z_right, 0)
            done(z_right)
            finish(far_0)
            far_1 = relay_x(zh + 3)
            far_2 = relay_x(zh + 1)
            got(z_far, 0)
            fan_x(z_far, 0)
            got(z_far, 1)
            fan_x(z_far, 1)
            done(z_far)
            finish(far_1)
            finish(far_2)
            finish(relay_x(zh + 2))

        return first, rest

    def nothing(*unused):
        return None

    def token_gather(chunk):
        def rows(start, size):
            return pl.ds(chunk * chunk_rows + start, size)

        def share(col):
            ref = toks.at[core, col, rows(0, chunk_rows)]
            push(ref, ref, p_sem.at[chunk, col], partner, c)

        first, rest = gather(
            lambda col, part: toks.at[core, col, rows(part * piece, piece)],
            t_sem.at[chunk],
            share,
        )

        def start():
            first()
            share(c)

        return start, rest

    tok = [token_gather(chunk) for chunk in range(CHUNKS)]
    tok[0][0]()
    held = first_ref.shape[0]
    unit_matrix = (
        lax.broadcasted_iota(jnp.int32, (RANK, RANK), 0)
        == lax.broadcasted_iota(jnp.int32, (RANK, RANK), 1)
    ).astype(jnp.bfloat16)
    for a in range(held):
        ad_own[pl.ds(a * RANK, RANK), :] = lax.dot_general(
            unit_matrix,
            first_ref[a],
            (((1,), (1,)), ((), ())),
            preferred_element_type=jnp.float32,
        ).astype(jnp.bfloat16)
        ad_own[pl.ds((held + a) * RANK, RANK), :] = second_ref[a]
    keep_own = pltpu.make_async_copy(ad_own, ad_all.at[core, half_row], local.at[1])
    keep_own.start()
    for i in row_steps:
        push(ad_own, ad_all.at[core, half_row], a_sem.at[half_row], 2 * i + core, c)
    units = gate_ref.shape[0]
    rows = down_ref[...].astype(jnp.float32)
    blank = jnp.zeros((units, width), jnp.float32)
    for parity in range(2):
        spread = []
        for col in range(n_col):
            mine = rows[col * units : (col + 1) * units]
            spread += [mine, blank] if parity == 0 else [blank, mine]
        wd[pl.ds(parity * width, width), :] = jnp.transpose(
            jnp.concatenate(spread, axis=0)
        ).astype(jnp.bfloat16)
    for k in range(1, RING):
        z = (zh + k) % RING
        arrived(gainz.at[z], gz_sem.at[z])
    keep = pltpu.make_async_copy(gainz, gainx.at[xx], local.at[3])
    keep.start()
    for p in (x_right, x_left, x_far):
        push(gainz, gainx.at[xx], gx_sem.at[xx], r, p)
    tok[0][1](tok[1][0])
    ones = jnp.ones((8, width), jnp.float32)
    keep.wait()
    for k in range(1, RING):
        x = (xx + k) % RING
        arrived(gainx.at[x], gx_sem.at[x])
    nil = jnp.zeros((UNITS_PAD - units, width), jnp.float32)
    for col in range(n_col):
        lanes = pl.ds(col * width, width)
        gain = gainx[col % RING, col // RING]
        wg[:, lanes] = jnp.concatenate(
            [
                gate_ref[:, lanes].astype(jnp.float32) * gain,
                nil,
                up_ref[:, lanes].astype(jnp.float32) * gain,
                nil,
            ],
            axis=0,
        ).astype(jnp.bfloat16)

    step = 256
    steps = chunk_rows // step
    part_steps = steps // 2
    features = n_col * width

    def hidden_of(chunk):
        for k in range(n_col):
            arrived(toks.at[other, k, pl.ds(chunk * chunk_rows, chunk_rows)], p_sem.at[chunk, k])

        def of_parity(parity, at):
            from_row = pl.multiple_of(chunk * chunk_rows + at, step)
            pieces = [toks[parity, col, pl.ds(from_row, step), :] for col in range(n_col)]
            squares = jnp.zeros((step, width), jnp.float32)
            for x in pieces:
                wide = x.astype(jnp.float32)
                squares = squares + wide * wide
            mean = lax.dot_general(
                ones,
                squares,
                (((1,), (1,)), ((), ())),
                precision=lax.Precision.HIGHEST,
                preferred_element_type=jnp.float32,
            )[0:1]
            both = lax.dot_general(
                wg[...],
                jnp.concatenate(pieces, axis=1),
                (((1,), (1,)), ((), ())),
                preferred_element_type=jnp.float32,
            ) * lax.rsqrt(mean / features + 1e-06)
            gate, up = both[:units], both[UNITS_PAD : UNITS_PAD + units]
            return gate / (1.0 + jnp.exp(-gate)) * up

        def one(k, carry):
            at = pl.multiple_of(k * step, step)
            in_part = pl.multiple_of((k % part_steps) * step, step)
            hid[chunk, c, k // part_steps, :, pl.ds(in_part, step)] = jnp.concatenate(
                [of_parity(0, at), of_parity(1, at)], axis=0
            ).astype(jnp.bfloat16)
            return carry

        lax.fori_loop(0, steps, one, 0)

    def hidden_gather(chunk):
        return gather(
            lambda col, part: hid.at[chunk, col, part], h_sem.at[chunk], nothing
        )

    def out_of(chunk):
        def one(k, carry):
            at = pl.multiple_of(k * step, step)
            in_part = pl.multiple_of((k % part_steps) * step, step)
            h = hid[chunk, :, k // part_steps, :, pl.ds(in_part, step)].reshape(n_col * 2 * units, step)
            y = jnp.dot(wd[...], h, preferred_element_type=jnp.float32)
            for parity in range(2):
                both_out[chunk, parity, pl.ds(at, step), :] = jnp.transpose(
                    y[parity * width : (parity + 1) * width]
                )
            return carry

        lax.fori_loop(0, steps, one, 0)
        osend[chunk] = both_out[chunk, other].astype(jnp.bfloat16)
        push(osend.at[chunk], orecv.at[chunk], o_sem.at[chunk], partner, c)

    def total_of(chunk):
        arrived(orecv.at[chunk], o_sem.at[chunk])
        rbuf[chunk] = (both_out[chunk, core] + orecv[chunk].astype(jnp.float32)).astype(jnp.bfloat16)

    hids = [hidden_gather(chunk) for chunk in range(CHUNKS)]
    hidden_of(0)
    hids[0][0]()
    for i in row_steps:
        arrived(ad_all.at[core, i], a_sem.at[i])
    keep_own.wait()
    push(ad_all.at[core], ad_all.at[core], ap_sem.at[0], partner, c)
    arrived(ad_all.at[other], ap_sem.at[0])
    wide = tok_ref[...].astype(jnp.float32)
    scaled = (wide * gain_ref[...]).astype(jnp.bfloat16)
    total = jnp.zeros((RANK, tok_ref.shape[0]), jnp.float32)
    for parity in range(2):
        factors = ad_all[parity, :, : held * RANK, :].reshape(pairs * held * RANK, width)
        part = lax.dot_general(
            factors, scaled, (((1,), (1,)), ((), ())), preferred_element_type=jnp.float32
        )
        at = lax.broadcasted_iota(jnp.int32, part.shape, 0) // RANK
        of = (2 * (at // held) + parity) * held + at % held
        part = jnp.where(of == adapter_ref[...], part, 0.0)
        total = total + jnp.sum(part.reshape(pairs * held, RANK, part.shape[1]), axis=0)
    low[pl.ds(0, RANK), :] = total
    low[pl.ds(RANK, 8), :] = lax.dot_general(
        ones,
        wide * wide,
        (((1,), (1,)), ((), ())),
        precision=lax.Precision.HIGHEST,
        preferred_element_type=jnp.float32,
    )
    for p in (z_right, z_left, z_far):
        push(low, lowz.at[zh], lz_sem.at[zh], r, p)
    tok[1][1](nothing)
    total = low[...]
    for k in range(1, RING):
        z = (zh + k) % RING
        arrived(lowz.at[z], lz_sem.at[z])
        total = total + lowz[z]
    lowmid[...] = total
    for p in (x_right, x_left, x_far):
        push(lowmid, lowx.at[xx], lx_sem.at[xx], r, p)
    hidden_of(1)
    hids[0][1](hids[1][0])
    for k in range(1, RING):
        x = (xx + k) % RING
        arrived(lowx.at[x], lx_sem.at[x])
        total = total + lowx[x]
    lowsum_ref[...] = total
    out_of(0)
    hids[1][1](nothing)
    total_of(0)
    out_of(1)
    total_of(1)
    per = pairs // CHUNKS

    def sums_of(i):
        return rbuf.at[i // per, pl.ds((i % per) * SLOTS, SLOTS)]

    back = pltpu.make_async_copy(sums_of(half_row), ret_ref.at[half_row], local.at[0])
    back.start()
    for i in row_steps:
        push(sums_of(i), ret_ref.at[half_row], r_sem.at[half_row], 2 * i + core, c)
    back.wait()
    for i in row_steps:
        arrived(ret_ref.at[i], r_sem.at[i])
    for copy in sends:
        copy.wait_send()


def main_exchange(
    buffer, tokens, adapter, gain, first, second, gate_rows, up_rows, down_rows, n_row, n_col
):
    pairs = n_row // 2
    rows_half = pairs * SLOTS
    chunk_rows = rows_half // CHUNKS
    width = buffer.shape[-1]
    low_shape = (RANK + 8, tokens.shape[0])
    units = gate_rows.shape[0]
    factors_shape = (2 * RANK * first.shape[0], width)
    dma = pltpu.SemaphoreType.DMA
    sends = 3 * (pairs - 1) + 1 + 12 + CHUNKS * (60 + n_col + 1)
    return pl.pallas_call(
        functools.partial(main_kernel, n_row),
        out_shape=(
            jax.ShapeDtypeStruct((pairs, SLOTS, width), jnp.bfloat16),
            jax.ShapeDtypeStruct(low_shape, jnp.float32),
            jax.ShapeDtypeStruct((2, pairs) + factors_shape, jnp.bfloat16),
        ),
        in_specs=[VMEM] * 9,
        out_specs=(VMEM,) * 3,
        scratch_shapes=[
            pltpu.VMEM((2, n_col, rows_half, width), jnp.bfloat16),
            pltpu.VMEM((CHUNKS, n_col, 2, 2 * units, chunk_rows // 2), jnp.bfloat16),
            pltpu.VMEM((2 * UNITS_PAD, n_col * width), jnp.bfloat16),
            pltpu.VMEM((2 * width, n_col * 2 * units), jnp.bfloat16),
            pltpu.VMEM(factors_shape, jnp.bfloat16),
            pltpu.VMEM(low_shape, jnp.float32),
            pltpu.VMEM((RING,) + low_shape, jnp.float32),
            pltpu.VMEM(low_shape, jnp.float32),
            pltpu.VMEM((RING,) + low_shape, jnp.float32),
            pltpu.VMEM((RING,) + gain.shape, jnp.float32),
            pltpu.VMEM((RING, RING) + gain.shape, jnp.float32),
            pltpu.VMEM((CHUNKS, chunk_rows, width), jnp.bfloat16),
            pltpu.VMEM((CHUNKS, chunk_rows, width), jnp.bfloat16),
            pltpu.VMEM((CHUNKS, 2, chunk_rows, width), jnp.float32),
            pltpu.VMEM((CHUNKS, chunk_rows, width), jnp.bfloat16),
            dma((sends,)),
            dma((4,)),
            dma((pairs,)),
            dma((CHUNKS, 2 * n_col)),
            dma((CHUNKS, n_col)),
            dma((CHUNKS, 2 * n_col)),
            dma((RING,)),
            dma((RING,)),
            dma((RING,)),
            dma((RING,)),
            dma((pairs,)),
            dma((1,)),
            dma((CHUNKS,)),
            dma((pairs,)),
        ],
        compiler_params=pltpu.CompilerParams(collective_id=1, has_side_effects=True),
    )(buffer, tokens, adapter, gain, first, second, gate_rows, up_rows, down_rows)


def body(
    tokens,
    norm_gain,
    lengths,
    request_adapter,
    routes,
    route_weights,
    gate_weight,
    up_weight,
    down_weight,
    adapter_down,
    adapter_up,
):
    tok_rows, width_part = tokens.shape
    n_row, n_col = lax.axis_size("row"), lax.axis_size("col")
    req_ends = jnp.cumsum(lengths)
    position = lax.axis_index("row") * tok_rows + jnp.arange(tok_rows, dtype=jnp.int32)
    request = jnp.sum((position[:, None] >= req_ends[None, :]).astype(jnp.int32), axis=1)
    request_hot = request[:, None] == jnp.arange(lengths.shape[0], dtype=jnp.int32)[None, :]
    adapter = jnp.sum(jnp.where(request_hot, request_adapter[None, :], 0), axis=1)
    adapter_count = adapter_down.shape[0] * n_row
    ranks = adapter_down.shape[0] * RANK
    rank_adapter = jnp.arange(adapter_count * RANK, dtype=jnp.int32) // RANK
    chosen = rank_adapter[:, None] == adapter[None, :]
    assigned = routes.reshape(-1)
    assign_count = assigned.shape[0]
    expert_hot = (assigned[:, None] == jnp.arange(EXPERTS, dtype=jnp.int32)[None, :]).astype(
        jnp.int32
    )
    earlier = (
        jnp.arange(assign_count, dtype=jnp.int32)[:, None]
        > jnp.arange(assign_count, dtype=jnp.int32)[None, :]
    )
    before = jnp.dot(
        earlier.astype(jnp.bfloat16),
        expert_hot.astype(jnp.bfloat16),
        preferred_element_type=jnp.float32,
    ).astype(jnp.int32)
    slot_index = jnp.sum(before * expert_hot, axis=1)
    placed_at = assigned * SLOTS + slot_index
    placing = (jnp.arange(EXPERTS * SLOTS, dtype=jnp.int32)[:, None] == placed_at[None, :]).astype(
        jnp.bfloat16
    )
    placing_token = jnp.sum(placing.reshape(EXPERTS * SLOTS, tok_rows, TOPK), axis=2)
    buffer = jnp.dot(placing_token, tokens, preferred_element_type=jnp.float32).astype(
        jnp.bfloat16
    )
    returned, low_sum, factors = main_exchange(
        buffer.reshape(EXPERTS, SLOTS, width_part),
        tokens,
        adapter[None, :],
        norm_gain[None, :],
        adapter_down,
        adapter_up,
        gate_weight[0],
        up_weight[0],
        down_weight[0],
        n_row,
        n_col,
    )
    scale = lax.rsqrt(low_sum[RANK] / D + 1e-06)
    low_rank = (low_sum[:RANK] * scale[None, :]).astype(jnp.bfloat16)
    up_rows = jnp.transpose(factors[:, :, ranks:], (1, 0, 2, 3)).reshape(
        adapter_count * RANK, width_part
    )
    expanded = jnp.where(
        chosen,
        jnp.broadcast_to(low_rank[None], (adapter_count, RANK, tok_rows)).reshape(
            adapter_count * RANK, tok_rows
        ),
        jnp.zeros((), jnp.bfloat16),
    )
    branch = lax.dot_general(
        expanded, up_rows, (((0,), (0,)), ((), ())), preferred_element_type=jnp.float32
    )
    twice = jnp.broadcast_to(
        placing.reshape(EXPERTS, 1, SLOTS, assign_count), (EXPERTS, 2, SLOTS, assign_count)
    ).reshape(EXPERTS * 2 * SLOTS, assign_count)
    gathered = lax.dot_general(
        twice,
        returned.reshape(EXPERTS * 2 * SLOTS, width_part),
        (((0,), (0,)), ((), ())),
        preferred_element_type=jnp.float32,
    )
    weighted = jnp.sum(
        gathered.reshape(tok_rows, TOPK, width_part) * route_weights[:, :, None], axis=1
    )
    return (weighted + branch).astype(jnp.bfloat16)


def solution(mesh):
    in_specs = (
        P("row", "col"),
        P("col"),
        P(),
        P(),
        P("row", None),
        P("row", None),
        P("row", "col", None),
        P("row", "col", None),
        P("row", None, "col"),
        P("row", "col", None),
        P("row", None, "col"),
    )
    out_specs = P("row", "col")
    return jax.shard_map(body, mesh=mesh, in_specs=in_specs, out_specs=out_specs, check_vma=False)
```

```python
import functools

import jax
import jax.numpy as jnp
from jax import lax
from jax.experimental import pallas as pl
from jax.experimental.pallas import tpu as pltpu
from jax.sharding import PartitionSpec as P

D = 2048
EXPERTS = 8
TOPK = 2
RANK = 16
CAP = 60
SLOTS = 64
RING = 4
UNITS_PAD = 96
MESH = pl.DeviceIdType.MESH
VMEM = pl.BlockSpec(memory_space=pltpu.VMEM)


def greet(peers):
    barrier = pltpu.get_barrier_semaphore()
    for row, col in peers:
        pl.semaphore_signal(barrier, inc=1, device_id=(row, col), device_id_type=MESH)
    pl.semaphore_wait(barrier, len(peers))


CHUNKS = 2


def main_kernel(
    n_row,
    buf_ref,
    tok_ref,
    adapter_ref,
    gain_ref,
    first_ref,
    second_ref,
    gate_ref,
    up_ref,
    down_ref,
    ret_ref,
    lowsum_ref,
    ad_all,
    toks,
    hid,
    wg,
    wd,
    ad_own,
    low,
    lowz,
    lowmid,
    lowx,
    gainz,
    gainx,
    osend,
    orecv,
    both_out,
    rbuf,
    send,
    local,
    d_sem,
    t_sem,
    p_sem,
    h_sem,
    lz_sem,
    lx_sem,
    gz_sem,
    gx_sem,
    a_sem,
    ap_sem,
    o_sem,
    r_sem,
):
    r, c = lax.axis_index("row"), lax.axis_index("col")
    core, half_row = r % 2, r // 2
    other = 1 - core
    partner = r + 1 - 2 * core
    zh, xx = c // RING, c % RING
    n_col = RING * RING
    pairs = n_row // 2
    rows_half = pairs * SLOTS
    chunk_rows = rows_half // CHUNKS
    piece = chunk_rows // 2
    width = buf_ref.shape[-1]

    def col_of(z, x):
        return (z % RING) * RING + x % RING

    z_right, z_left, z_far = col_of(zh + 1, xx), col_of(zh + 3, xx), col_of(zh + 2, xx)
    x_right, x_left, x_far = col_of(zh, xx + 1), col_of(zh, xx + 3), col_of(zh, xx + 2)
    row_steps = [(half_row + k) % pairs for k in range(1, pairs)]
    greet(
        [(2 * i + core, c) for i in row_steps]
        + [(r, p) for p in (z_right, z_left, z_far, x_right, x_left, x_far)]
        + [(partner, c)]
    )
    sends = []

    def push(src, dst, recv, row, col):
        copy = pltpu.make_async_remote_copy(
            src, dst, send.at[len(sends)], recv, (row, col), MESH
        )
        copy.start()
        sends.append(copy)

    def arrived(ref, recv):
        pltpu.make_async_copy(ref, ref, recv).wait()

    def expert_of(i):
        return (2 * i + core) // 4

    own = [
        pltpu.make_async_copy(
            buf_ref.at[expert_of(half_row)],
            toks.at[core, c, pl.ds(half_row * SLOTS, SLOTS)],
            local.at[0],
        ),
        pltpu.make_async_copy(gain_ref, gainz.at[zh], local.at[2]),
    ]
    for copy in own:
        copy.start()
    for i in row_steps:
        push(
            buf_ref.at[expert_of(i)],
            toks.at[core, c, pl.ds(half_row * SLOTS, SLOTS)],
            d_sem.at[half_row],
            2 * i + core,
            c,
        )
    for p in (z_right, z_left, z_far):
        push(gain_ref, gainz.at[zh], gz_sem.at[zh], r, p)
    for copy in own:
        copy.wait()
    for i in row_steps:
        arrived(toks.at[core, c, pl.ds(i * SLOTS, SLOTS)], d_sem.at[i])

    def gather(piece_of, sem, done):
        def go(col, part, to):
            push(piece_of(col, part), piece_of(col, part), sem.at[col * 2 + part], r, to)

        def got(col, part):
            arrived(piece_of(col, part), sem.at[col * 2 + part])

        def fan_x(col, part):
            go(col, part, x_right)
            go(col, part, x_left)

        def relay_x(z):
            from_left, from_right, far = col_of(z, xx + 3), col_of(z, xx + 1), col_of(z, xx + 2)
            got(from_left, 0)
            go(from_left, 0, x_right)
            got(from_right, 1)
            go(from_right, 1, x_left)
            got(from_left, 1)
            done(from_left)
            got(from_right, 0)
            done(from_right)
            return far

        def finish(far):
            got(far, 0)
            got(far, 1)
            done(far)

        def first():
            for part in range(2):
                go(c, part, z_right)
                go(c, part, z_left)
                fan_x(c, part)

        def rest(after_z):
            far_0 = relay_x(zh)
            got(z_left, 0)
            go(z_left, 0, z_right)
            fan_x(z_left, 0)
            got(z_right, 1)
            go(z_right, 1, z_left)
            fan_x(z_right, 1)
            got(z_left, 1)
            fan_x(z_left, 1)
            done(z_left)
            got(z_right, 0)
            fan_x(z_right, 0)
            done(z_right)
            after_z()
            finish(far_0)
            far_1 = relay_x(zh + 3)
            far_2 = relay_x(zh + 1)
            got(z_far, 0)
            fan_x(z_far, 0)
            got(z_far, 1)
            fan_x(z_far, 1)
            done(z_far)
            finish(far_1)
            finish(far_2)
            finish(relay_x(zh + 2))

        return first, rest

    def nothing(*unused):
        return None

    def token_gather(chunk):
        def rows(start, size):
            return pl.ds(chunk * chunk_rows + start, size)

        def share(col):
            ref = toks.at[core, col, rows(0, chunk_rows)]
            push(ref, ref, p_sem.at[chunk, col], partner, c)

        first, rest = gather(
            lambda col, part: toks.at[core, col, rows(part * piece, piece)],
            t_sem.at[chunk],
            share,
        )

        def start():
            first()
            share(c)

        return start, rest

    tok = [token_gather(chunk) for chunk in range(CHUNKS)]
    tok[0][0]()
    held = first_ref.shape[0]
    unit_matrix = (
        lax.broadcasted_iota(jnp.int32, (RANK, RANK), 0)
        == lax.broadcasted_iota(jnp.int32, (RANK, RANK), 1)
    ).astype(jnp.bfloat16)
    for a in range(held):
        ad_own[pl.ds(a * RANK, RANK), :] = lax.dot_general(
            unit_matrix,
            first_ref[a],
            (((1,), (1,)), ((), ())),
            preferred_element_type=jnp.float32,
        ).astype(jnp.bfloat16)
        ad_own[pl.ds((held + a) * RANK, RANK), :] = second_ref[a]
    keep_own = pltpu.make_async_copy(ad_own, ad_all.at[core, half_row], local.at[1])
    keep_own.start()
    for i in row_steps:
        push(ad_own, ad_all.at[core, half_row], a_sem.at[half_row], 2 * i + core, c)
    units = gate_ref.shape[0]
    rows = down_ref[...].astype(jnp.float32)
    blank = jnp.zeros((units, width), jnp.float32)
    for parity in range(2):
        spread = []
        for col in range(n_col):
            mine = rows[col * units : (col + 1) * units]
            spread += [mine, blank] if parity == 0 else [blank, mine]
        wd[pl.ds(parity * width, width), :] = jnp.transpose(
            jnp.concatenate(spread, axis=0)
        ).astype(jnp.bfloat16)
    for k in range(1, RING):
        z = (zh + k) % RING
        arrived(gainz.at[z], gz_sem.at[z])
    keep = pltpu.make_async_copy(gainz, gainx.at[xx], local.at[3])
    keep.start()
    for p in (x_right, x_left, x_far):
        push(gainz, gainx.at[xx], gx_sem.at[xx], r, p)
    tok[0][1](tok[1][0])
    ones = jnp.ones((8, width), jnp.float32)
    keep.wait()
    for k in range(1, RING):
        x = (xx + k) % RING
        arrived(gainx.at[x], gx_sem.at[x])
    nil = jnp.zeros((UNITS_PAD - units, width), jnp.float32)
    for col in range(n_col):
        lanes = pl.ds(col * width, width)
        gain = gainx[col % RING, col // RING]
        wg[:, lanes] = jnp.concatenate(
            [
                gate_ref[:, lanes].astype(jnp.float32) * gain,
                nil,
                up_ref[:, lanes].astype(jnp.float32) * gain,
                nil,
            ],
            axis=0,
        ).astype(jnp.bfloat16)

    step = 256
    steps = chunk_rows // step
    part_steps = steps // 2
    features = n_col * width

    def hidden_of(chunk):
        for k in range(n_col):
            arrived(toks.at[other, k, pl.ds(chunk * chunk_rows, chunk_rows)], p_sem.at[chunk, k])

        def of_parity(parity, at):
            from_row = pl.multiple_of(chunk * chunk_rows + at, step)
            pieces = [toks[parity, col, pl.ds(from_row, step), :] for col in range(n_col)]
            squares = jnp.zeros((step, width), jnp.float32)
            for x in pieces:
                wide = x.astype(jnp.float32)
                squares = squares + wide * wide
            mean = lax.dot_general(
                ones,
                squares,
                (((1,), (1,)), ((), ())),
                precision=lax.Precision.HIGHEST,
                preferred_element_type=jnp.float32,
            )[0:1]
            both = lax.dot_general(
                wg[...],
                jnp.concatenate(pieces, axis=1),
                (((1,), (1,)), ((), ())),
                preferred_element_type=jnp.float32,
            ) * lax.rsqrt(mean / features + 1e-06)
            gate, up = both[:units], both[UNITS_PAD : UNITS_PAD + units]
            return gate / (1.0 + jnp.exp(-gate)) * up

        def one(k, carry):
            at = pl.multiple_of(k * step, step)
            in_part = pl.multiple_of((k % part_steps) * step, step)
            hid[chunk, c, k // part_steps, :, pl.ds(in_part, step)] = jnp.concatenate(
                [of_parity(0, at), of_parity(1, at)], axis=0
            ).astype(jnp.bfloat16)
            return carry

        lax.fori_loop(0, steps, one, 0)

    def hidden_gather(chunk):
        return gather(
            lambda col, part: hid.at[chunk, col, part], h_sem.at[chunk], nothing
        )

    def out_of(chunk):
        def one(k, carry):
            at = pl.multiple_of(k * step, step)
            in_part = pl.multiple_of((k % part_steps) * step, step)
            h = hid[chunk, :, k // part_steps, :, pl.ds(in_part, step)].reshape(n_col * 2 * units, step)
            y = jnp.dot(wd[...], h, preferred_element_type=jnp.float32)
            for parity in range(2):
                both_out[chunk, parity, pl.ds(at, step), :] = jnp.transpose(
                    y[parity * width : (parity + 1) * width]
                )
            return carry

        lax.fori_loop(0, steps, one, 0)
        osend[chunk] = both_out[chunk, other].astype(jnp.bfloat16)
        push(osend.at[chunk], orecv.at[chunk], o_sem.at[chunk], partner, c)

    def total_of(chunk):
        arrived(orecv.at[chunk], o_sem.at[chunk])
        rbuf[chunk] = (both_out[chunk, core] + orecv[chunk].astype(jnp.float32)).astype(jnp.bfloat16)

    hids = [hidden_gather(chunk) for chunk in range(CHUNKS)]
    hidden_of(0)
    hids[0][0]()
    for i in row_steps:
        arrived(ad_all.at[core, i], a_sem.at[i])
    keep_own.wait()
    push(ad_all.at[core], ad_all.at[core], ap_sem.at[0], partner, c)
    arrived(ad_all.at[other], ap_sem.at[0])
    wide = tok_ref[...].astype(jnp.float32)
    scaled = (wide * gain_ref[...]).astype(jnp.bfloat16)
    total = jnp.zeros((RANK, tok_ref.shape[0]), jnp.float32)
    for parity in range(2):
        factors = ad_all[parity, :, : held * RANK, :].reshape(pairs * held * RANK, width)
        part = lax.dot_general(
            factors, scaled, (((1,), (1,)), ((), ())), preferred_element_type=jnp.float32
        )
        at = lax.broadcasted_iota(jnp.int32, part.shape, 0) // RANK
        of = (2 * (at // held) + parity) * held + at % held
        part = jnp.where(of == adapter_ref[...], part, 0.0)
        total = total + jnp.sum(part.reshape(pairs * held, RANK, part.shape[1]), axis=0)
    low[pl.ds(0, RANK), :] = total
    low[pl.ds(RANK, 8), :] = lax.dot_general(
        ones,
        wide * wide,
        (((1,), (1,)), ((), ())),
        precision=lax.Precision.HIGHEST,
        preferred_element_type=jnp.float32,
    )
    for p in (z_right, z_left, z_far):
        push(low, lowz.at[zh], lz_sem.at[zh], r, p)
    tok[1][1](nothing)
    total = low[...]
    for k in range(1, RING):
        z = (zh + k) % RING
        arrived(lowz.at[z], lz_sem.at[z])
        total = total + lowz[z]
    lowmid[...] = total
    for p in (x_right, x_left, x_far):
        push(lowmid, lowx.at[xx], lx_sem.at[xx], r, p)
    hidden_of(1)
    hids[0][1](hids[1][0])
    for k in range(1, RING):
        x = (xx + k) % RING
        arrived(lowx.at[x], lx_sem.at[x])
        total = total + lowx[x]
    lowsum_ref[...] = total
    out_of(0)
    hids[1][1](nothing)
    total_of(0)
    out_of(1)
    total_of(1)
    per = pairs // CHUNKS

    def sums_of(i):
        return rbuf.at[i // per, pl.ds((i % per) * SLOTS, SLOTS)]

    back = pltpu.make_async_copy(sums_of(half_row), ret_ref.at[half_row], local.at[0])
    back.start()
    for i in row_steps:
        push(sums_of(i), ret_ref.at[half_row], r_sem.at[half_row], 2 * i + core, c)
    back.wait()
    for i in row_steps:
        arrived(ret_ref.at[i], r_sem.at[i])
    for copy in sends:
        copy.wait_send()


def main_exchange(
    buffer, tokens, adapter, gain, first, second, gate_rows, up_rows, down_rows, n_row, n_col
):
    pairs = n_row // 2
    rows_half = pairs * SLOTS
    chunk_rows = rows_half // CHUNKS
    width = buffer.shape[-1]
    low_shape = (RANK + 8, tokens.shape[0])
    units = gate_rows.shape[0]
    factors_shape = (2 * RANK * first.shape[0], width)
    dma = pltpu.SemaphoreType.DMA
    sends = 3 * (pairs - 1) + 1 + 12 + CHUNKS * (60 + n_col + 1)
    return pl.pallas_call(
        functools.partial(main_kernel, n_row),
        out_shape=(
            jax.ShapeDtypeStruct((pairs, SLOTS, width), jnp.bfloat16),
            jax.ShapeDtypeStruct(low_shape, jnp.float32),
            jax.ShapeDtypeStruct((2, pairs) + factors_shape, jnp.bfloat16),
        ),
        in_specs=[VMEM] * 9,
        out_specs=(VMEM,) * 3,
        scratch_shapes=[
            pltpu.VMEM((2, n_col, rows_half, width), jnp.bfloat16),
            pltpu.VMEM((CHUNKS, n_col, 2, 2 * units, chunk_rows // 2), jnp.bfloat16),
            pltpu.VMEM((2 * UNITS_PAD, n_col * width), jnp.bfloat16),
            pltpu.VMEM((2 * width, n_col * 2 * units), jnp.bfloat16),
            pltpu.VMEM(factors_shape, jnp.bfloat16),
            pltpu.VMEM(low_shape, jnp.float32),
            pltpu.VMEM((RING,) + low_shape, jnp.float32),
            pltpu.VMEM(low_shape, jnp.float32),
            pltpu.VMEM((RING,) + low_shape, jnp.float32),
            pltpu.VMEM((RING,) + gain.shape, jnp.float32),
            pltpu.VMEM((RING, RING) + gain.shape, jnp.float32),
            pltpu.VMEM((CHUNKS, chunk_rows, width), jnp.bfloat16),
            pltpu.VMEM((CHUNKS, chunk_rows, width), jnp.bfloat16),
            pltpu.VMEM((CHUNKS, 2, chunk_rows, width), jnp.float32),
            pltpu.VMEM((CHUNKS, chunk_rows, width), jnp.bfloat16),
            dma((sends,)),
            dma((4,)),
            dma((pairs,)),
            dma((CHUNKS, 2 * n_col)),
            dma((CHUNKS, n_col)),
            dma((CHUNKS, 2 * n_col)),
            dma((RING,)),
            dma((RING,)),
            dma((RING,)),
            dma((RING,)),
            dma((pairs,)),
            dma((1,)),
            dma((CHUNKS,)),
            dma((pairs,)),
        ],
        compiler_params=pltpu.CompilerParams(collective_id=1, has_side_effects=True),
    )(buffer, tokens, adapter, gain, first, second, gate_rows, up_rows, down_rows)


def body(
    tokens,
    norm_gain,
    lengths,
    request_adapter,
    routes,
    route_weights,
    gate_weight,
    up_weight,
    down_weight,
    adapter_down,
    adapter_up,
):
    tok_rows, width_part = tokens.shape
    n_row, n_col = lax.axis_size("row"), lax.axis_size("col")
    req_ends = jnp.cumsum(lengths)
    position = lax.axis_index("row") * tok_rows + jnp.arange(tok_rows, dtype=jnp.int32)
    request = jnp.sum((position[:, None] >= req_ends[None, :]).astype(jnp.int32), axis=1)
    request_hot = request[:, None] == jnp.arange(lengths.shape[0], dtype=jnp.int32)[None, :]
    adapter = jnp.sum(jnp.where(request_hot, request_adapter[None, :], 0), axis=1)
    adapter_count = adapter_down.shape[0] * n_row
    ranks = adapter_down.shape[0] * RANK
    rank_adapter = jnp.arange(adapter_count * RANK, dtype=jnp.int32) // RANK
    chosen = rank_adapter[:, None] == adapter[None, :]
    assigned = routes.reshape(-1)
    assign_count = assigned.shape[0]
    expert_hot = (assigned[:, None] == jnp.arange(EXPERTS, dtype=jnp.int32)[None, :]).astype(
        jnp.int32
    )
    earlier = (
        jnp.arange(assign_count, dtype=jnp.int32)[:, None]
        > jnp.arange(assign_count, dtype=jnp.int32)[None, :]
    )
    before = jnp.dot(
        earlier.astype(jnp.bfloat16),
        expert_hot.astype(jnp.bfloat16),
        preferred_element_type=jnp.float32,
    ).astype(jnp.int32)
    slot_index = jnp.sum(before * expert_hot, axis=1)
    placed_at = assigned * SLOTS + slot_index
    placing = (jnp.arange(EXPERTS * SLOTS, dtype=jnp.int32)[:, None] == placed_at[None, :]).astype(
        jnp.bfloat16
    )
    placing_token = jnp.sum(placing.reshape(EXPERTS * SLOTS, tok_rows, TOPK), axis=2)
    buffer = jnp.dot(placing_token, tokens, preferred_element_type=jnp.float32).astype(
        jnp.bfloat16
    )
    returned, low_sum, factors = main_exchange(
        buffer.reshape(EXPERTS, SLOTS, width_part),
        tokens,
        adapter[None, :],
        norm_gain[None, :],
        adapter_down,
        adapter_up,
        gate_weight[0],
        up_weight[0],
        down_weight[0],
        n_row,
        n_col,
    )
    scale = lax.rsqrt(low_sum[RANK] / D + 1e-06)
    low_rank = (low_sum[:RANK] * scale[None, :]).astype(jnp.bfloat16)
    up_rows = jnp.transpose(factors[:, :, ranks:], (1, 0, 2, 3)).reshape(
        adapter_count * RANK, width_part
    )
    expanded = jnp.where(
        chosen,
        jnp.broadcast_to(low_rank[None], (adapter_count, RANK, tok_rows)).reshape(
            adapter_count * RANK, tok_rows
        ),
        jnp.zeros((), jnp.bfloat16),
    )
    branch = lax.dot_general(
        expanded, up_rows, (((0,), (0,)), ((), ())), preferred_element_type=jnp.float32
    )
    twice = jnp.broadcast_to(
        placing.reshape(EXPERTS, 1, SLOTS, assign_count), (EXPERTS, 2, SLOTS, assign_count)
    ).reshape(EXPERTS * 2 * SLOTS, assign_count)
    gathered = lax.dot_general(
        twice,
        returned.reshape(EXPERTS * 2 * SLOTS, width_part),
        (((0,), (0,)), ((), ())),
        preferred_element_type=jnp.float32,
    )
    weighted = jnp.sum(
        gathered.reshape(tok_rows, TOPK, width_part) * route_weights[:, :, None], axis=1
    )
    return (weighted + branch).astype(jnp.bfloat16)


def solution(mesh):
    in_specs = (
        P("row", "col"),
        P("col"),
        P(),
        P(),
        P("row", None),
        P("row", None),
        P("row", "col", None),
        P("row", "col", None),
        P("row", None, "col"),
        P("row", "col", None),
        P("row", None, "col"),
    )
    out_specs = P("row", "col")
    return jax.shard_map(body, mesh=mesh, in_specs=in_specs, out_specs=out_specs, check_vma=False)
```
